32 devices in a mesh: freq: 4 (over x, core), tm: 8 (over z, y).
Axes of the slice: x: 2, y: 2, z: 4, core: 2. Of those that a mesh axis runs over, the one named last changes fastest.
Arguments:
- visibilities: float32 [8, 8, 1024], P('freq', None, 'tm'), may hold values from -6 to 6
- coherencies: bfloat16 [8, 8, 8, 1024], P('freq', None, None, 'tm'), may hold values from -2.09375 to 2.09375
- pairs: int32 [2, 1024], P(None, 'tm'), may hold values from 0 to 511, as said below
- gains_start: float32 [8, 8, 8, 512], P('freq'), may hold values from -0.9 to 1.9
- duals_start: float32 [8, 8, 8, 512], P('freq'), may hold values from -12 to 12
- poly_start: float32 [4, 8, 8, 512], replicated, may hold values from -0.6 to 1.6
Outputs:
- gains: float32 [8, 8, 8, 512], P('freq')
- duals: float32 [8, 8, 8, 512], P('freq')
- polynomial: float32 [4, 8, 8, 512], replicated
The draws below stay inside these ranges and needn't reach their ends.
Inputs may be any that keep to these rules, and one draw needn't show every extreme that they name: `pairs`: each row names two different stations.
All inputs are finite; a program needn't handle non-finite values.
Results may differ from the reference program's by a relative error of at most 0.0003.
Values sent between devices are 32-bit elements; how exact they have to be, the bound alone decides.
A program may use at most 64 MiB of HBM per device.

```python
from functools import partial
import jax
import jax.numpy as jnp
from jax import lax

STATIONS = 512
DIRS = 8
POLY = 4
ITERS = 2
STEPS = 1
NCHAN = 8
ROWS_ALL = 1024


def identity_mask():
    index = jnp.arange(8)
    return ((index == 0) | (index == 3)).astype(jnp.float32)[None, :, None, None]


def draw_pairs(key, part):
    first_key, second_key = jax.random.split(jax.random.fold_in(key, 11))
    first = jax.random.randint(first_key, (ROWS_ALL,), 0, STATIONS)
    offset = jax.random.randint(second_key, (ROWS_ALL,), 1, STATIONS)
    second = (first + offset) % STATIONS
    return jnp.stack([first, second]).astype(jnp.int32)


def draw_gains_start(key, part):
    noise_key = jax.random.fold_in(jax.random.fold_in(key, 23), 0)
    shape = (NCHAN, 8, DIRS, STATIONS)
    noise = 0.3 * jnp.clip(jax.random.normal(noise_key, shape, jnp.float32), -3.0, 3.0)
    return noise + identity_mask()


def draw_poly_start(key, part):
    noise_key = jax.random.fold_in(jax.random.fold_in(key, 37), 0)
    shape = (POLY, 8, DIRS, STATIONS)
    noise = 0.2 * jnp.clip(jax.random.normal(noise_key, shape, jnp.float32), -3.0, 3.0)
    leading = (jnp.arange(POLY) == 0).astype(jnp.float32)[:, None, None, None]
    return noise + leading * identity_mask()


def block_levels(own_key, extent, pieces, low, largest):
    def one(dim, shards_of):
        heights = jax.random.uniform(jax.random.fold_in(jax.random.fold_in(own_key, 6), dim), (shards_of,), jnp.float32, low / len(pieces), largest / len(pieces))
        return jnp.repeat(jnp.exp(heights), extent[dim] // shards_of).reshape((-1,) + (1,) * (len(extent) - dim - 1))

    gain = one(*pieces[0])
    for cut in pieces[1:]:
        gain = gain * one(*cut)
    return gain


def normal_values(stream_key, dims, scale, most, cuts=(), kind=jnp.bfloat16):
    entries = jax.random.normal(stream_key, dims, jnp.float32) * scale
    if len(cuts) > 0:
        entries = block_levels(stream_key, dims, cuts, -0.22, 0.18) * entries
    return jnp.clip(entries, min=-most, max=most).astype(kind)


def setup_inputs(seed: int = 0) -> dict:
    splits = jax.random.split(jax.random.key(seed), 7)
    return {
        "visibilities": normal_values(splits[0], (NCHAN, 8, ROWS_ALL), 1.0, 6.0, ((0, 4), (2, 8)), jnp.float32),
        "coherencies": normal_values(splits[1], (NCHAN, 8, DIRS, ROWS_ALL), 0.35, 2.09375, ((0, 4), (3, 8))),
        "pairs": draw_pairs(jax.random.fold_in(splits[6], 71), 0),
        "gains_start": draw_gains_start(jax.random.fold_in(splits[6], 71), 0),
        "duals_start": normal_values(splits[4], (NCHAN, 8, DIRS, STATIONS), 2.0, 12.0, ((0, 4),), jnp.float32),
        "poly_start": draw_poly_start(jax.random.fold_in(splits[6], 71), 0),
    }


RHO = 16.0
HIGHEST = lax.Precision.HIGHEST

def split(block):
    return ([block[i] for i in range(4)], [block[i + 4] for i in range(4)])

def join(matrix):
    return jnp.stack(matrix[0] + matrix[1])

def adjoint(matrix):
    real_part, imag_part = matrix
    return ([real_part[0], real_part[2], real_part[1], real_part[3]], [-imag_part[0], -imag_part[2], -imag_part[1], -imag_part[3]])

def product(left, right):
    left_real, left_imag = left
    right_real, right_imag = right
    out_real = []
    out_imag = []
    for row in range(2):
        for column in range(2):
            first = 2 * row
            out_real.append(left_real[first] * right_real[column] - left_imag[first] * right_imag[column] + left_real[first + 1] * right_real[column + 2] - left_imag[first + 1] * right_imag[column + 2])
            out_imag.append(left_real[first] * right_imag[column] + left_imag[first] * right_real[column] + left_real[first + 1] * right_imag[column + 2] + left_imag[first + 1] * right_real[column + 2])
    return (out_real, out_imag)

def normal(matrix):
    real_part, imag_part = matrix
    top_left = real_part[0] ** 2 + imag_part[0] ** 2 + real_part[1] ** 2 + imag_part[1] ** 2
    bottom_right = real_part[2] ** 2 + imag_part[2] ** 2 + real_part[3] ** 2 + imag_part[3] ** 2
    cross_real = real_part[0] * real_part[2] + imag_part[0] * imag_part[2] + real_part[1] * real_part[3] + imag_part[1] * imag_part[3]
    cross_imag = imag_part[0] * real_part[2] - real_part[0] * imag_part[2] + imag_part[1] * real_part[3] - real_part[1] * imag_part[3]
    return jnp.stack([top_left, bottom_right, cross_real, cross_imag])

def data_sums(gains, coherencies, visibilities, pairs):
    jones_first = split(jnp.take(gains, pairs[0], axis=2))
    jones_second = split(jnp.take(gains, pairs[1], axis=2))
    skymodel = split(coherencies.astype(jnp.float32))
    left = product(jones_first, skymodel)
    right = product(skymodel, adjoint(jones_second))
    model = jnp.sum(join(product(left, adjoint(jones_second))), axis=1)
    residual = split((visibilities - model)[:, None, :])
    first_terms = jnp.concatenate([join(product(residual, adjoint(right))), normal(right)], axis=0)
    second_terms = jnp.concatenate([join(product(adjoint(residual), left)), normal(adjoint(left))], axis=0)
    terms = jnp.concatenate([first_terms, second_terms], axis=2)
    stations = jnp.concatenate([pairs[0], pairs[1]]).astype(jnp.int32)
    flat = terms.reshape(-1, terms.shape[2]).T
    summed = jax.ops.segment_sum(flat, stations, num_segments=gains.shape[2])
    return summed.T.reshape(12, gains.shape[1], gains.shape[2])

def update(gains, duals, prior, sums, damping):
    direction = split(sums[:8] - duals - RHO * (gains - prior))
    top_left, bottom_right, cross_real, cross_imag = (sums[8], sums[9], sums[10], sums[11])
    shift = damping * 0.5 * (top_left + bottom_right) + RHO
    upper = top_left + shift
    lower = bottom_right + shift
    determinant = upper * lower - cross_real * cross_real - cross_imag * cross_imag
    zeros = jnp.zeros_like(determinant)
    inverse = ([lower / determinant, -cross_real / determinant, -cross_real / determinant, upper / determinant], [zeros, -cross_imag / determinant, cross_imag / determinant, zeros])
    return gains + join(product(direction, inverse))

def basis_weights(count):
    position = (2.0 * jnp.arange(count).astype(jnp.float32) + 1.0) / count - 1.0
    basis = jnp.stack([jnp.ones_like(position), position, 1.5 * position * position - 0.5, 2.5 * position * position * position - 1.5 * position], axis=1)
    gram = jnp.dot(basis.T, basis, precision=HIGHEST)
    factor = jnp.linalg.cholesky(gram)
    weights = jax.scipy.linalg.cho_solve((factor, True), basis.T)
    return (basis, weights)

def reference(visibilities, coherencies, pairs, gains_start, duals_start, poly_start):
    basis, weights = basis_weights(gains_start.shape[0])
    prior = jnp.einsum('fj,jcks->fcks', basis, poly_start, precision=HIGHEST)
    gains, duals, polynomial = (gains_start, duals_start, poly_start)

    def channel(items):
        return data_sums(items[0], items[1], items[2], pairs)
    for outer in range(STEPS):
        for inner in range(ITERS):
            sums = lax.map(channel, (gains, coherencies, visibilities))
            gains = jax.vmap(partial(update, damping=12.0 * 0.5 ** inner))(gains, duals, prior, sums)
        mixed = gains + duals / RHO
        polynomial = jnp.einsum('jf,fcks->jcks', weights, mixed, precision=HIGHEST)
        prior = jnp.einsum('fj,jcks->fcks', basis, polynomial, precision=HIGHEST)
        duals = duals + RHO * (gains - prior)
    return (gains, duals, polynomial)
```

```python
from functools import partial

import jax
import jax.numpy as jnp
import numpy as np
from jax import lax
from jax.experimental import pallas as pl
from jax.experimental.pallas import tpu as pltpu
from jax.sharding import PartitionSpec as P

ITERS = 2
RHO = 16.0
LANES = 128
OUTER = 4


def split(block):
    return ([block[i] for i in range(4)], [block[i + 4] for i in range(4)])


def product(left, right):
    lr, li = left
    rr, ri = right
    out_real, out_imag = [], []
    for row in range(2):
        for col in range(2):
            a, b = 2 * row, 2 * row + 1
            out_real.append(lr[a] * rr[col] - li[a] * ri[col] + lr[b] * rr[col + 2] - li[b] * ri[col + 2])
            out_imag.append(lr[a] * ri[col] + li[a] * rr[col] + lr[b] * ri[col + 2] + li[b] * rr[col + 2])
    return (out_real, out_imag)


def product_right_adjoint(left, right):
    lr, li = left
    rr, ri = right
    out_real, out_imag = [], []
    for row in range(2):
        for col in range(2):
            a, b, c, d = 2 * row, 2 * row + 1, 2 * col, 2 * col + 1
            out_real.append(lr[a] * rr[c] + li[a] * ri[c] + lr[b] * rr[d] + li[b] * ri[d])
            out_imag.append(li[a] * rr[c] - lr[a] * ri[c] + li[b] * rr[d] - lr[b] * ri[d])
    return (out_real, out_imag)


def product_left_adjoint(left, right):
    lr, li = left
    rr, ri = right
    out_real, out_imag = [], []
    for row in range(2):
        for col in range(2):
            a, b, c, d = row, row + 2, col, col + 2
            out_real.append(lr[a] * rr[c] + li[a] * ri[c] + lr[b] * rr[d] + li[b] * ri[d])
            out_imag.append(lr[a] * ri[c] - li[a] * rr[c] + lr[b] * ri[d] - li[b] * rr[d])
    return (out_real, out_imag)


def normal(r, i, rows):
    (a, b), (c, d) = rows
    top = r[a] * r[a] + i[a] * i[a] + r[b] * r[b] + i[b] * i[b]
    bottom = r[c] * r[c] + i[c] * i[c] + r[d] * r[d] + i[d] * i[d]
    real = r[a] * r[c] + i[a] * i[c] + r[b] * r[d] + i[b] * i[d]
    imag = i[a] * r[c] - r[a] * i[c] + i[b] * r[d] - r[b] * i[d]
    return top, bottom, real, imag


def basis_weights(count):
    x = (2.0 * np.arange(count, dtype=np.float64) + 1.0) / count - 1.0
    basis = np.stack([np.ones_like(x), x, 1.5 * x * x - 0.5, 2.5 * x * x * x - 1.5 * x], axis=1)
    return np.linalg.solve(basis.T @ basis, basis.T)


def halves(value):
    high = value.astype(jnp.bfloat16)
    return high, (value - high.astype(jnp.float32)).astype(jnp.bfloat16)


def from_basis(bases, f, coefficients):
    total = coefficients[0]
    for j in range(1, len(coefficients)):
        total = total + bases[f][j] * coefficients[j]
    return total


def local_bases(F, nf):
    bases = []
    for f in range(F):
        channel = (lax.axis_index("freq") * F + f).astype(jnp.float32)
        x = (2.0 * channel + 1.0) / (F * nf) - 1.0
        bases.append([None, x, 1.5 * x * x - 0.5, 2.5 * x * x * x - 1.5 * x])
    return bases


ORDER = ((1, 2, 3), (0, 2, 3), (1, 3, 0), (2, 1, 0))


def store_kernel(*refs):
    count = len(refs) // 2
    sem = refs[-1]
    copies = [pltpu.make_async_copy(refs[i], refs[count + i], sem.at[i]) for i in range(count)]
    for copy in copies:
        copy.start()
    for copy in copies:
        copy.wait()


def kernel(cfg, vis_hbm, coh_hbm, pairs_hbm, gains_hbm, duals_hbm, poly_hbm,
           gains_out, duals_out, poly_out,
           mixed, data, hot, tall, terms, jones, taken, pull, vis_ref, coh_ref, pairs_ref, gains_ref, duals_ref, poly_ref,
           tm_send, tm_recv, far, fq_send, fq_recv, load_sem):
    F, K, S, nt, nf, inner, chunks, terms_poly = cfg
    CH = S // chunks
    C = 8 * K
    tm = lax.axis_index("tm")
    fq = lax.axis_index("freq")
    z, y = tm // inner, tm % inner
    partner = fq + 1 - 2 * (fq % 2)
    MESH = pl.DeviceIdType.MESH
    columns_apart = range(1, inner)
    others = range(1, nf // 2)

    def ordered(k):
        found = ORDER[0][k]
        for i in range(1, OUTER):
            found = jnp.where(z == i, ORDER[i][k], found)
        return found

    nth = [ordered(k) for k in range(OUTER - 1)]

    def at(row, e):
        return row * inner + (y + e) % inner

    def across(fq, d):
        there = (fq + 2 * d) % nf
        return there + 1 - 2 * (there % 2)

    barrier = pltpu.get_barrier_semaphore()

    def greet(peer):
        pl.semaphore_signal(barrier, inc=1, device_id=peer, device_id_type=MESH)

    for k in range(OUTER - 1):

        @pl.when((z < OUTER - 1) | (nth[k] == OUTER - 2))
        def _():
            greet({"tm": at(nth[k], 0)})

    for e in columns_apart:
        greet({"tm": at(z, e)})
    greet({"freq": partner})
    for d in others:
        greet({"freq": across(fq, d)})

    loads = [pltpu.make_async_copy(src, dst, load_sem.at[i]) for i, (src, dst) in enumerate(
        ((coh_hbm, coh_ref), (vis_hbm, vis_ref), (pairs_hbm, pairs_ref),
         (gains_hbm, gains_ref), (duals_hbm, duals_ref), (poly_hbm, poly_ref)))]
    for load in loads:
        load.start()
    pl.semaphore_wait(barrier, jnp.where(z < OUTER - 2, OUTER - 2, OUTER - 1) + (inner - 1) + 1 + (nf // 2 - 1))
    for low in range(OUTER - 2):

        @pl.when(z == OUTER - 1)
        def _():
            pl.semaphore_signal(far, inc=1, device_id={"tm": at(low, 0)}, device_id_type=MESH)

    for load in loads[:3]:
        load.wait()
    data[tm, 0, 0:8, :] = jnp.zeros((8, LANES), jnp.float32)
    data[tm, 0, 0:2, :] = pairs_ref[...].astype(jnp.float32)
    for f in range(F):
        data[tm, f, 8:16, :] = vis_ref[f]
        data[tm, f, 16:, :] = coh_ref[f].astype(jnp.float32).reshape(C, LANES)

    def tm_copy(block, f, slot, device):
        rows = pl.ds(0, 16 + C) if f == 0 else pl.ds(8, 8 + C)
        return pltpu.make_async_remote_copy(
            src_ref=data.at[block, f, rows], dst_ref=data.at[block, f, rows],
            send_sem=tm_send.at[slot, f], recv_sem=tm_recv.at[block, f],
            device_id={"tm": device}, device_id_type=MESH)

    def arrived(block, f):
        tm_copy(block, f, 0, at(z, 1)).wait_recv()

    sends = []

    def send(block, f, slot, device):
        copy = tm_copy(block, f, slot, device)
        copy.start()
        sends.append(copy)

    def relay(row, f, place):
        for e in columns_apart:
            send(at(row, 0), f, OUTER - 1 + place * inner + e, at(z, e))

    def direct(k, f):
        send(tm, f, k, at(nth[k], 0))

    stations = lax.broadcasted_iota(jnp.int32, (S, LANES), 0).astype(jnp.float32)

    across_stations = lax.broadcasted_iota(jnp.int32, (LANES, S), 1).astype(jnp.float32)

    def columns(block, half):
        at_row = block * 2 * LANES + half * LANES
        return pl.ds(at_row if isinstance(at_row, int) else pl.multiple_of(at_row, LANES), LANES)

    def make_hot(block):
        for half in range(2):
            row = data[block, 0, half : half + 1, :]
            hot[:, columns(block, half)] = jnp.where(stations == row, 1.0, 0.0).astype(jnp.bfloat16)
        turned = data[block, 0, 0:8, :].T
        for half in range(2):
            tall[columns(block, half), :] = jnp.where(across_stations == turned[:, half : half + 1], 1.0, 0.0).astype(jnp.bfloat16)

    def load_gains(gains, f):
        high, low = halves(gains[f].reshape(C, S))
        jones[2 * f * C : (2 * f + 1) * C, :] = high
        jones[(2 * f + 1) * C : (2 * f + 2) * C, :] = low

    def gather(block, first, last):
        at_row = block * 2 * LANES
        both = pl.ds(at_row if isinstance(at_row, int) else pl.multiple_of(at_row, 2 * LANES), 2 * LANES)
        found = jnp.dot(jones[2 * first * C : 2 * last * C, :], hot[:, both], preferred_element_type=jnp.float32)
        for f in range(first, last):
            base = 2 * (f - first) * C
            taken[block, f] = found[base : base + C] + found[base + C : base + 2 * C]

    def rows_sums(block, f):
        first = split([taken[block, f, c * K : (c + 1) * K, :LANES] for c in range(8)])
        second = split([taken[block, f, c * K : (c + 1) * K, LANES:] for c in range(8)])
        sky = split([data[block, f, 16 + c * K : 16 + (c + 1) * K, :] for c in range(8)])
        left = product(first, sky)
        right = product_right_adjoint(sky, second)
        model = product_right_adjoint(left, second)
        model = model[0] + model[1]
        residual = []
        for c in range(8):
            seen = data[block, f, 8 + c : 9 + c, :]
            residual.append(jnp.broadcast_to(seen - jnp.sum(model[c], axis=0, keepdims=True), (K, LANES)))
        residual = split(residual)
        ends = []
        out = product_right_adjoint(residual, right)
        ends.append(out[0] + out[1] + list(normal(right[0], right[1], ((0, 1), (2, 3)))))
        out = product_left_adjoint(residual, left)
        top, bottom, real, imag = normal(left[0], left[1], ((0, 2), (1, 3)))
        ends.append(out[0] + out[1] + [top, bottom, real, -imag])
        for half in range(2):
            high, low = halves(jnp.concatenate(ends[half], axis=0))
            terms[f, : 12 * K, columns(block, half)] = high
            terms[f, 12 * K :, columns(block, half)] = low

    bases = local_bases(F, nf)

    def pulls(f):
        for c in range(8):
            prior = from_basis(bases, f, [poly_ref[j, c] for j in range(terms_poly)])
            pull[f, c] = RHO * prior - duals_ref[f, c]

    def update(source, f, damping, chunk):
        lanes = slice(chunk * CH, (chunk + 1) * CH)
        sums = jnp.dot(terms[f], tall[:, lanes], preferred_element_type=jnp.float32)
        sums = sums[: 12 * K] + sums[12 * K :]
        part = [sums[c * K : (c + 1) * K] for c in range(12)]
        old, step = [], []
        for c in range(8):
            gain = source[f, c, :, lanes]
            old.append(gain)
            step.append(part[c] + pull[f, c, :, lanes] - RHO * gain)
        top, bottom, real, imag = part[8:]
        shift = damping * 0.5 * (top + bottom) + RHO
        upper, lower = top + shift, bottom + shift
        scale = 1.0 / (upper * lower - real * real - imag * imag)
        a, d, br, bi = lower * scale, upper * scale, -real * scale, -imag * scale
        sr, si = split(step)
        for row in range(2):
            p, q = 2 * row, 2 * row + 1
            gains_out[f, p, :, lanes] = old[p] + sr[p] * a + sr[q] * br + si[q] * bi
            gains_out[f, p + 4, :, lanes] = old[p + 4] + si[p] * a + si[q] * br - sr[q] * bi
            gains_out[f, q, :, lanes] = old[q] + sr[p] * br - si[p] * bi + sr[q] * d
            gains_out[f, q + 4, :, lanes] = old[q + 4] + si[p] * br + sr[p] * bi + si[q] * d

    def take(block, f):
        if f == 0:
            make_hot(block)
            gather(block, 0, F)
        rows_sums(block, f)

    def fq_copy(owner, f, chunk, slot, device):
        return pltpu.make_async_remote_copy(
            src_ref=mixed.at[owner, f, chunk], dst_ref=mixed.at[owner, f, chunk],
            send_sem=fq_send.at[slot, f, chunk], recv_sem=fq_recv.at[owner, f, chunk],
            device_id={"freq": device}, device_id_type=MESH)

    def fq_start(owner, f, chunk, slot, device):
        copy = fq_copy(owner, f, chunk, slot, device)
        copy.start()
        sends.append(copy)

    def finish(f):
        for chunk in range(chunks):
            update(gains_ref, f, 12.0, chunk)
        for step in range(1, ITERS):
            load_gains(gains_out, f)

            for block in range(nt):
                gather(block, f, f + 1)
            for block in range(nt):
                rows_sums(block, f)

            for chunk in range(chunks):
                update(gains_out, f, 12.0 * 0.5**step, chunk)
                if step == ITERS - 1:
                    lanes = slice(chunk * CH, (chunk + 1) * CH)
                    value = gains_out[f, :, :, lanes] + duals_ref[f, :, :, lanes] * (1.0 / RHO)
                    mixed[fq, f, chunk] = value.reshape(C, CH)
                    for d in others:
                        fq_start(fq, f, chunk, d, across(fq, d))
                    fq_start(fq, f, chunk, 0, partner)

    def forward(f):
        for chunk in range(chunks):
            for d in others:
                owner = across(fq, nf // 2 - d)
                fq_copy(owner, f, chunk, 0, partner).wait_recv()
                fq_start(owner, f, chunk, nf // 2 + d, partner)

    weights = basis_weights(F * nf)

    def received(f, chunk):
        fq_copy(partner, f, chunk, 0, partner).wait_recv()
        for d in others:
            fq_copy(across(partner, nf // 2 - d), f, chunk, 0, partner).wait_recv()

    def fit(f, chunk):
        lanes = slice(chunk * CH, (chunk + 1) * CH)
        for c in range(8):
            values = [mixed[n, f, chunk, c * K : (c + 1) * K, :] for n in range(nf)]
            coefficients = []
            for j in range(terms_poly):
                total = float(weights[j, f]) * values[0]
                for n in range(1, nf):
                    total = total + float(weights[j, n * F + f]) * values[n]
                if f > 0:
                    total = total + poly_out[j, c, :, lanes]
                poly_out[j, c, :, lanes] = total
                coefficients.append(total)
            if f == F - 1:
                for g in range(F):
                    prior = from_basis(bases, g, coefficients)
                    duals_out[g, c, :, lanes] = duals_ref[g, c, :, lanes] + RHO * (gains_out[g, c, :, lanes] - prior)

    later = range(1, F)
    for f in range(F):
        direct(0, f)
        relay(z, f, 0)
        direct(1, f)
        last = tm_copy(tm, f, 2, at(nth[2], 0))
        sends.append(last)

        @pl.when(z >= OUTER - 2)
        def _():
            last.start()

    loads[3].wait()
    for f in range(F):
        load_gains(gains_ref, f)
    for f in range(F):
        take(tm, f)

    @pl.when(z < OUTER - 2)
    def _():
        pl.semaphore_wait(far, 1)
        for f in range(F):
            tm_copy(tm, f, 2, at(nth[2], 0)).start()

    loads[4].wait()
    loads[5].wait()
    for f in range(F):
        pulls(f)

    def column(k, f):
        arrived(at(nth[k], 0), f)
        relay(nth[k], f, k + 1)
        take(at(nth[k], 0), f)

    def aside(row, f):
        for e in columns_apart:
            arrived(at(row, e), f)
            take(at(row, e), f)

    aside(z, 0)
    column(0, 0)
    for f in later:
        aside(z, f)
    column(1, 0)
    aside(nth[0], 0)
    for f in later:
        column(0, f)
    column(2, 0)
    for f in later:
        column(1, f)
    aside(nth[1], 0)
    for f in later:
        column(2, f)
        aside(nth[0], f)
    aside(nth[2], 0)
    finish(0)
    for f in later:
        aside(nth[1], f)
        aside(nth[2], f)
        finish(f)
        forward(f - 1)
        for chunk in range(chunks):
            received(f - 1, chunk)
            fit(f - 1, chunk)
    forward(F - 1)
    for chunk in range(chunks):
        received(F - 1, chunk)
        fit(F - 1, chunk)
    for copy in sends:
        copy.wait_send()


def solution(mesh):
    nt, nf = mesh.shape["tm"], mesh.shape["freq"]

    def shards(*operands):
        visibilities, coherencies, pairs, gains_start, _, poly_start = operands
        F, _, K, S = gains_start.shape
        inner = nt // OUTER
        chunks = 2
        C = 8 * K
        CH = S // chunks
        cfg = (F, K, S, nt, nf, inner, chunks, poly_start.shape[0])
        wide = lambda x: pltpu.VMEM(x.shape, jnp.float32)
        vmem = pl.BlockSpec(memory_space=pltpu.VMEM)
        hbm = pl.BlockSpec(memory_space=pltpu.HBM)
        results = (gains_start, gains_start, poly_start)
        shapes = tuple(jax.ShapeDtypeStruct(x.shape, jnp.float32) for x in results)
        held = pl.pallas_call(
            partial(kernel, cfg),
            out_shape=shapes,
            in_specs=[hbm] * 6,
            out_specs=(vmem,) * 3,
            scratch_shapes=[
                pltpu.VMEM((nf, F, chunks, C, CH), jnp.float32),
                pltpu.VMEM((nt, F, 16 + C, LANES), jnp.float32),
                pltpu.VMEM((S, nt * 2 * LANES), jnp.bfloat16),
                pltpu.VMEM((nt * 2 * LANES, S), jnp.bfloat16),
                pltpu.VMEM((F, 2 * 12 * K, nt * 2 * LANES), jnp.bfloat16),
                pltpu.VMEM((2 * F * C, S), jnp.bfloat16),
                pltpu.VMEM((nt, F, C, 2 * LANES), jnp.float32),
                wide(gains_start),
                pltpu.VMEM(visibilities.shape, jnp.float32),
                pltpu.VMEM(coherencies.shape, jnp.bfloat16),
                pltpu.VMEM(pairs.shape, jnp.int32),
                wide(gains_start),
                wide(gains_start),
                wide(poly_start),
                pltpu.SemaphoreType.DMA((OUTER - 1 + OUTER * inner, F)),
                pltpu.SemaphoreType.DMA((nt, F)),
                pltpu.SemaphoreType.REGULAR,
                pltpu.SemaphoreType.DMA((nf + 1, F, chunks)),
                pltpu.SemaphoreType.DMA((nf, F, chunks)),
                pltpu.SemaphoreType.DMA((6,)),
            ],
            compiler_params=pltpu.CompilerParams(collective_id=0, has_side_effects=True,
                                                 vmem_limit_bytes=40 * 2**20),
        )(*(pltpu.with_memory_space_constraint(x, pltpu.HBM) for x in operands))
        return pl.pallas_call(
            store_kernel,
            out_shape=shapes,
            in_specs=[vmem] * 3,
            out_specs=(hbm,) * 3,
            scratch_shapes=[pltpu.SemaphoreType.DMA((3,))],
            compiler_params=pltpu.CompilerParams(vmem_limit_bytes=16 * 2**20),
        )(*held)

    placed = (
        P("freq", None, "tm"),
        P("freq", None, None, "tm"),
        P(None, "tm"),
        P("freq", None, None, None),
        P("freq", None, None, None),
        P(),
    )
    return jax.shard_map(
        shards,
        mesh=mesh,
        in_specs=placed,
        out_specs=(P("freq", None, None, None), P("freq", None, None, None), P()),
        check_vma=False,
    )
```

```python
from functools import partial

import jax
import jax.numpy as jnp
import numpy as np
from jax import lax
from jax.experimental import pallas as pl
from jax.experimental.pallas import tpu as pltpu
from jax.sharding import PartitionSpec as P

ITERS = 2
RHO = 16.0
LANES = 128
OUTER = 4


def split(block):
    return ([block[i] for i in range(4)], [block[i + 4] for i in range(4)])


def product(left, right):
    lr, li = left
    rr, ri = right
    out_real, out_imag = [], []
    for row in range(2):
        for col in range(2):
            a, b = 2 * row, 2 * row + 1
            out_real.append(lr[a] * rr[col] - li[a] * ri[col] + lr[b] * rr[col + 2] - li[b] * ri[col + 2])
            out_imag.append(lr[a] * ri[col] + li[a] * rr[col] + lr[b] * ri[col + 2] + li[b] * rr[col + 2])
    return (out_real, out_imag)


def product_right_adjoint(left, right):
    lr, li = left
    rr, ri = right
    out_real, out_imag = [], []
    for row in range(2):
        for col in range(2):
            a, b, c, d = 2 * row, 2 * row + 1, 2 * col, 2 * col + 1
            out_real.append(lr[a] * rr[c] + li[a] * ri[c] + lr[b] * rr[d] + li[b] * ri[d])
            out_imag.append(li[a] * rr[c] - lr[a] * ri[c] + li[b] * rr[d] - lr[b] * ri[d])
    return (out_real, out_imag)


def product_left_adjoint(left, right):
    lr, li = left
    rr, ri = right
    out_real, out_imag = [], []
    for row in range(2):
        for col in range(2):
            a, b, c, d = row, row + 2, col, col + 2
            out_real.append(lr[a] * rr[c] + li[a] * ri[c] + lr[b] * rr[d] + li[b] * ri[d])
            out_imag.append(lr[a] * ri[c] - li[a] * rr[c] + lr[b] * ri[d] - li[b] * rr[d])
    return (out_real, out_imag)


def normal(r, i, rows):
    (a, b), (c, d) = rows
    top = r[a] * r[a] + i[a] * i[a] + r[b] * r[b] + i[b] * i[b]
    bottom = r[c] * r[c] + i[c] * i[c] + r[d] * r[d] + i[d] * i[d]
    real = r[a] * r[c] + i[a] * i[c] + r[b] * r[d] + i[b] * i[d]
    imag = i[a] * r[c] - r[a] * i[c] + i[b] * r[d] - r[b] * i[d]
    return top, bottom, real, imag


def basis_weights(count):
    x = (2.0 * np.arange(count, dtype=np.float64) + 1.0) / count - 1.0
    basis = np.stack([np.ones_like(x), x, 1.5 * x * x - 0.5, 2.5 * x * x * x - 1.5 * x], axis=1)
    return np.linalg.solve(basis.T @ basis, basis.T)


def halves(value):
    high = value.astype(jnp.bfloat16)
    return high, (value - high.astype(jnp.float32)).astype(jnp.bfloat16)


def from_basis(bases, f, coefficients):
    total = coefficients[0]
    for j in range(1, len(coefficients)):
        total = total + bases[f][j] * coefficients[j]
    return total


def local_bases(F, nf):
    bases = []
    for f in range(F):
        channel = (lax.axis_index("freq") * F + f).astype(jnp.float32)
        x = (2.0 * channel + 1.0) / (F * nf) - 1.0
        bases.append([None, x, 1.5 * x * x - 0.5, 2.5 * x * x * x - 1.5 * x])
    return bases


SOURCES = ((1, 3, 2), (0, 2, 3), (1, 0, 3), (2, 0, 1))
FIRST = (
    ((1, 0), (0, 1), (2, 0)),
    ((0, 0), (1, 1), (2, 0)),
    ((1, 0), (2, 1), (3, 0)),
    ((0, 0), (3, 1), (1, 0), (2, 0)),
)
AFTER = (((3, 0),), (), (), ())
RELAYS = (
    {1: ((0, 1),), 3: ((0, 1),)},
    {2: ((0, 0), (1, 1), (0, 1)), 0: ((1, 1),), 3: ((1, 1),)},
    {1: ((3, 0), (2, 1)), 0: ((2, 1),), 3: ((2, 1),)},
    {2: ((3, 1),), 0: ((3, 1),), 1: ((3, 1),)},
)


def spread(targets, inner):
    return [(row, e) for row, aside in targets for e in (range(1, inner) if aside else (0,))]


def targets_of(row, inner):
    near = set(spread(FIRST[row], inner))
    for found in RELAYS[row].values():
        near |= set(spread(found, inner))
    return near


def store_kernel(*refs):
    count = len(refs) // 2
    sem = refs[-1]
    copies = [pltpu.make_async_copy(refs[i], refs[count + i], sem.at[i]) for i in range(count)]
    for copy in copies:
        copy.start()
    for copy in copies:
        copy.wait()


def kernel(cfg, vis_hbm, coh_hbm, pairs_hbm, gains_hbm, duals_hbm, poly_hbm,
           gains_out, duals_out, poly_out,
           mixed, data, hot, tall, terms, jones, taken, pull, vis_ref, coh_ref, pairs_ref, gains_ref, duals_ref, poly_ref,
           tm_send, tm_recv, far, fq_send, fq_recv, load_sem):
    F, K, S, nt, nf, inner, chunks, terms_poly = cfg
    CH = S // chunks
    C = 8 * K
    tm = lax.axis_index("tm")
    fq = lax.axis_index("freq")
    z, y = tm // inner, tm % inner
    partner = fq + 1 - 2 * (fq % 2)
    MESH = pl.DeviceIdType.MESH
    columns_apart = range(1, inner)
    others = range(1, nf // 2)

    def role(act):
        for row in range(OUTER):
            pl.when(z == row)(lambda row=row: act(row))

    def chosen(table):
        found = table[0]
        for row in range(1, OUTER):
            found = jnp.where(z == row, table[row], found)
        return found

    nth = [chosen([SOURCES[row][k] for row in range(OUTER)]) for k in range(OUTER - 1)]

    def at(row, e):
        return row * inner + (y + e) % inner

    def across(fq, d):
        there = (fq + 2 * d) % nf
        return there + 1 - 2 * (there % 2)

    barrier = pltpu.get_barrier_semaphore()

    def greet(peer):
        pl.semaphore_signal(barrier, inc=1, device_id=peer, device_id_type=MESH)

    def greet_rows(row):
        for other in range(OUTER):
            for there, e in sorted(targets_of(other, inner)):
                if there == row:
                    greet({"tm": at(other, inner - e)})

    role(greet_rows)
    greet({"freq": partner})
    for d in others:
        greet({"freq": across(fq, d)})

    loads = [pltpu.make_async_copy(src, dst, load_sem.at[i]) for i, (src, dst) in enumerate(
        ((coh_hbm, coh_ref), (vis_hbm, vis_ref), (pairs_hbm, pairs_ref),
         (gains_hbm, gains_ref), (duals_hbm, duals_ref), (poly_hbm, poly_ref)))]
    for load in loads:
        load.start()
    near = chosen([len(targets_of(row, inner)) for row in range(OUTER)])
    pl.semaphore_wait(barrier, near + 1 + (nf // 2 - 1))

    def greet_far(row):
        for other in range(OUTER):
            for there, _ in AFTER[other]:
                if there == row:
                    pl.semaphore_signal(far, inc=1, device_id={"tm": at(other, 0)}, device_id_type=MESH)

    role(greet_far)
    for load in loads[:3]:
        load.wait()
    data[tm, 0, 0:8, :] = jnp.zeros((8, LANES), jnp.float32)
    data[tm, 0, 0:2, :] = pairs_ref[...].astype(jnp.float32)
    for f in range(F):
        data[tm, f, 8:16, :] = vis_ref[f]
        data[tm, f, 16:, :] = coh_ref[f].astype(jnp.float32).reshape(C, LANES)

    def tm_copy(block, f, slot, device):
        rows = pl.ds(0, 16 + C) if f == 0 else pl.ds(8, 8 + C)
        return pltpu.make_async_remote_copy(
            src_ref=data.at[block, f, rows], dst_ref=data.at[block, f, rows],
            send_sem=tm_send.at[slot], recv_sem=tm_recv.at[block, f],
            device_id={"tm": device}, device_id_type=MESH)

    def arrived(block, f):
        tm_copy(block, f, 0, at(z, 1)).wait_recv()

    sends = []
    row_sends = [[] for _ in range(OUTER)]

    def send(row, source, f, targets):
        for there, e in spread(targets, inner):
            tm_copy(at(source, 0), f, len(row_sends[row]), at(there, e)).start()
            row_sends[row].append((source, f, there, e))

    def accept(group, f):
        def act(row):
            source, aside = (row, 1) if group == "mates" else (SOURCES[row][group[1]], group[0])
            for _, e in spread(((source, aside),), inner):
                arrived(at(source, e), f)
                if not aside:
                    send(row, source, f, relays(row, source, f))

        role(act)

    def relays(row, source, f):
        return RELAYS[row].get(source, ())

    stations = lax.broadcasted_iota(jnp.int32, (S, LANES), 0).astype(jnp.float32)

    across_stations = lax.broadcasted_iota(jnp.int32, (LANES, S), 1).astype(jnp.float32)

    def columns(block, half):
        at_row = block * 2 * LANES + half * LANES
        return pl.ds(at_row if isinstance(at_row, int) else pl.multiple_of(at_row, LANES), LANES)

    def make_hot(block):
        for half in range(2):
            row = data[block, 0, half : half + 1, :]
            hot[:, columns(block, half)] = jnp.where(stations == row, 1.0, 0.0).astype(jnp.bfloat16)
        turned = data[block, 0, 0:8, :].T
        for half in range(2):
            tall[columns(block, half), :] = jnp.where(across_stations == turned[:, half : half + 1], 1.0, 0.0).astype(jnp.bfloat16)

    def load_gains(gains, f):
        high, low = halves(gains[f].reshape(C, S))
        jones[2 * f * C : (2 * f + 1) * C, :] = high
        jones[(2 * f + 1) * C : (2 * f + 2) * C, :] = low

    def gather(block, first, last):
        at_row = block * 2 * LANES
        both = pl.ds(at_row if isinstance(at_row, int) else pl.multiple_of(at_row, 2 * LANES), 2 * LANES)
        found = jnp.dot(jones[2 * first * C : 2 * last * C, :], hot[:, both], preferred_element_type=jnp.float32)
        for f in range(first, last):
            base = 2 * (f - first) * C
            taken[block, f] = found[base : base + C] + found[base + C : base + 2 * C]

    def rows_sums(block, f):
        first = split([taken[block, f, c * K : (c + 1) * K, :LANES] for c in range(8)])
        second = split([taken[block, f, c * K : (c + 1) * K, LANES:] for c in range(8)])
        sky = split([data[block, f, 16 + c * K : 16 + (c + 1) * K, :] for c in range(8)])
        left = product(first, sky)
        right = product_right_adjoint(sky, second)
        model = product_right_adjoint(left, second)
        model = model[0] + model[1]
        residual = []
        for c in range(8):
            seen = data[block, f, 8 + c : 9 + c, :]
            residual.append(jnp.broadcast_to(seen - jnp.sum(model[c], axis=0, keepdims=True), (K, LANES)))
        residual = split(residual)
        ends = []
        out = product_right_adjoint(residual, right)
        ends.append(out[0] + out[1] + list(normal(right[0], right[1], ((0, 1), (2, 3)))))
        out = product_left_adjoint(residual, left)
        top, bottom, real, imag = normal(left[0], left[1], ((0, 2), (1, 3)))
        ends.append(out[0] + out[1] + [top, bottom, real, -imag])
        for half in range(2):
            high, low = halves(jnp.concatenate(ends[half], axis=0))
            terms[f, : 12 * K, columns(block, half)] = high
            terms[f, 12 * K :, columns(block, half)] = low

    bases = local_bases(F, nf)

    def pulls(f):
        for c in range(8):
            prior = from_basis(bases, f, [poly_ref[j, c] for j in range(terms_poly)])
            pull[f, c] = RHO * prior - duals_ref[f, c]

    def update(source, f, damping, chunk):
        lanes = slice(chunk * CH, (chunk + 1) * CH)
        sums = jnp.dot(terms[f], tall[:, lanes], preferred_element_type=jnp.float32)
        sums = sums[: 12 * K] + sums[12 * K :]
        part = [sums[c * K : (c + 1) * K] for c in range(12)]
        old, step = [], []
        for c in range(8):
            gain = source[f, c, :, lanes]
            old.append(gain)
            step.append(part[c] + pull[f, c, :, lanes] - RHO * gain)
        top, bottom, real, imag = part[8:]
        shift = damping * 0.5 * (top + bottom) + RHO
        upper, lower = top + shift, bottom + shift
        scale = 1.0 / (upper * lower - real * real - imag * imag)
        a, d, br, bi = lower * scale, upper * scale, -real * scale, -imag * scale
        sr, si = split(step)
        for row in range(2):
            p, q = 2 * row, 2 * row + 1
            gains_out[f, p, :, lanes] = old[p] + sr[p] * a + sr[q] * br + si[q] * bi
            gains_out[f, p + 4, :, lanes] = old[p + 4] + si[p] * a + si[q] * br - sr[q] * bi
            gains_out[f, q, :, lanes] = old[q] + sr[p] * br - si[p] * bi + sr[q] * d
            gains_out[f, q + 4, :, lanes] = old[q + 4] + si[p] * br + sr[p] * bi + si[q] * d

    def take(block, f):
        if f == 0:
            make_hot(block)
            gather(block, 0, F)
        rows_sums(block, f)

    def fq_copy(owner, f, chunk, slot, device):
        return pltpu.make_async_remote_copy(
            src_ref=mixed.at[owner, f, chunk], dst_ref=mixed.at[owner, f, chunk],
            send_sem=fq_send.at[slot, f, chunk], recv_sem=fq_recv.at[owner, f, chunk],
            device_id={"freq": device}, device_id_type=MESH)

    def fq_start(owner, f, chunk, slot, device):
        copy = fq_copy(owner, f, chunk, slot, device)
        copy.start()
        sends.append(copy)

    def finish(f):
        for chunk in range(chunks):
            update(gains_ref, f, 12.0, chunk)
        for step in range(1, ITERS):
            load_gains(gains_out, f)

            for block in range(nt):
                gather(block, f, f + 1)
            for block in range(nt):
                rows_sums(block, f)

            for chunk in range(chunks):
                update(gains_out, f, 12.0 * 0.5**step, chunk)
                if step == ITERS - 1:
                    lanes = slice(chunk * CH, (chunk + 1) * CH)
                    value = gains_out[f, :, :, lanes] + duals_ref[f, :, :, lanes] * (1.0 / RHO)
                    mixed[fq, f, chunk] = value.reshape(C, CH)
                    for d in others:
                        fq_start(fq, f, chunk, d, across(fq, d))
                    fq_start(fq, f, chunk, 0, partner)

    def forward(f):
        for chunk in range(chunks):
            for d in others:
                owner = across(fq, nf // 2 - d)
                fq_copy(owner, f, chunk, 0, partner).wait_recv()
                fq_start(owner, f, chunk, nf // 2 + d, partner)

    weights = basis_weights(F * nf)

    def received(f, chunk):
        fq_copy(partner, f, chunk, 0, partner).wait_recv()
        for d in others:
            fq_copy(across(partner, nf // 2 - d), f, chunk, 0, partner).wait_recv()

    def fit(f, chunk):
        lanes = slice(chunk * CH, (chunk + 1) * CH)
        for c in range(8):
            values = [mixed[n, f, chunk, c * K : (c + 1) * K, :] for n in range(nf)]
            coefficients = []
            for j in range(terms_poly):
                total = float(weights[j, f]) * values[0]
                for n in range(1, nf):
                    total = total + float(weights[j, n * F + f]) * values[n]
                if f > 0:
                    total = total + poly_out[j, c, :, lanes]
                poly_out[j, c, :, lanes] = total
                coefficients.append(total)
            if f == F - 1:
                for g in range(F):
                    prior = from_basis(bases, g, coefficients)
                    duals_out[g, c, :, lanes] = duals_ref[g, c, :, lanes] + RHO * (gains_out[g, c, :, lanes] - prior)

    later = range(1, F)
    def send_first(row):
        for f in range(F):
            send(row, row, f, FIRST[row])

    role(send_first)

    loads[3].wait()
    for f in range(F):
        load_gains(gains_ref, f)
    for f in range(F):
        take(tm, f)

    def send_after(row):
        if AFTER[row]:
            pl.semaphore_wait(far, len(AFTER[row]))
            for f in range(F):
                send(row, row, f, AFTER[row])

    role(send_after)
    loads[4].wait()
    loads[5].wait()
    for f in range(F):
        pulls(f)

    line = lambda k: (0, k)
    side = lambda k: (1, k)
    arrivals = [("mates", 0), (line(0), 0), (line(1), 0)]
    for f in later:
        arrivals += [("mates", f), (line(0), f), (line(1), f)]
    arrivals += [(side(0), 0), (line(2), 0)]
    for f in later:
        arrivals += [(line(2), f)]
    arrivals += [(side(1), 0)]
    for f in later:
        arrivals += [(side(0), f)]
    arrivals += [(side(2), 0)]
    for f in later:
        arrivals += [(side(1), f), (side(2), f)]

    def have(group, f):
        while (group, f) in arrivals:
            accept(*arrivals.pop(0))
        source, aside = (z, 1) if group == "mates" else (nth[group[1]], group[0])
        for _, e in spread(((0, aside),), inner):
            take(at(source, e), f)

    have("mates", 0)
    have(line(0), 0)
    have(line(1), 0)
    for f in later:
        have("mates", f)
        have(line(0), f)
        have(line(1), f)
    have(side(0), 0)
    have(line(2), 0)
    have(side(1), 0)
    have(side(2), 0)
    finish(0)
    for f in later:
        have(line(2), f)
        have(side(0), f)
        have(side(1), f)
        have(side(2), f)
        finish(f)
        forward(f - 1)
        for chunk in range(chunks):
            received(f - 1, chunk)
            fit(f - 1, chunk)
    forward(F - 1)
    for chunk in range(chunks):
        received(F - 1, chunk)
        fit(F - 1, chunk)
    for copy in sends:
        copy.wait_send()

    def drain(row):
        for slot, (source, f, there, e) in enumerate(row_sends[row]):
            tm_copy(at(source, 0), f, slot, at(there, e)).wait_send()

    role(drain)


def solution(mesh):
    nt, nf = mesh.shape["tm"], mesh.shape["freq"]

    def shards(*operands):
        visibilities, coherencies, pairs, gains_start, _, poly_start = operands
        F, _, K, S = gains_start.shape
        inner = nt // OUTER
        chunks = 2
        C = 8 * K
        CH = S // chunks
        cfg = (F, K, S, nt, nf, inner, chunks, poly_start.shape[0])
        wide = lambda x: pltpu.VMEM(x.shape, jnp.float32)
        vmem = pl.BlockSpec(memory_space=pltpu.VMEM)
        hbm = pl.BlockSpec(memory_space=pltpu.HBM)
        results = (gains_start, gains_start, poly_start)
        shapes = tuple(jax.ShapeDtypeStruct(x.shape, jnp.float32) for x in results)
        held = pl.pallas_call(
            partial(kernel, cfg),
            out_shape=shapes,
            in_specs=[hbm] * 6,
            out_specs=(vmem,) * 3,
            scratch_shapes=[
                pltpu.VMEM((nf, F, chunks, C, CH), jnp.float32),
                pltpu.VMEM((nt, F, 16 + C, LANES), jnp.float32),
                pltpu.VMEM((S, nt * 2 * LANES), jnp.bfloat16),
                pltpu.VMEM((nt * 2 * LANES, S), jnp.bfloat16),
                pltpu.VMEM((F, 2 * 12 * K, nt * 2 * LANES), jnp.bfloat16),
                pltpu.VMEM((2 * F * C, S), jnp.bfloat16),
                pltpu.VMEM((nt, F, C, 2 * LANES), jnp.float32),
                wide(gains_start),
                pltpu.VMEM(visibilities.shape, jnp.float32),
                pltpu.VMEM(coherencies.shape, jnp.bfloat16),
                pltpu.VMEM(pairs.shape, jnp.int32),
                wide(gains_start),
                wide(gains_start),
                wide(poly_start),
                pltpu.SemaphoreType.DMA((2 * OUTER * inner * F,)),
                pltpu.SemaphoreType.DMA((nt, F)),
                pltpu.SemaphoreType.REGULAR,
                pltpu.SemaphoreType.DMA((nf + 1, F, chunks)),
                pltpu.SemaphoreType.DMA((nf, F, chunks)),
                pltpu.SemaphoreType.DMA((6,)),
            ],
            compiler_params=pltpu.CompilerParams(collective_id=0, has_side_effects=True,
                                                 vmem_limit_bytes=40 * 2**20),
        )(*(pltpu.with_memory_space_constraint(x, pltpu.HBM) for x in operands))
        return pl.pallas_call(
            store_kernel,
            out_shape=shapes,
            in_specs=[vmem] * 3,
            out_specs=(hbm,) * 3,
            scratch_shapes=[pltpu.SemaphoreType.DMA((3,))],
            compiler_params=pltpu.CompilerParams(vmem_limit_bytes=16 * 2**20),
        )(*held)

    placed = (
        P("freq", None, "tm"),
        P("freq", None, None, "tm"),
        P(None, "tm"),
        P("freq", None, None, None),
        P("freq", None, None, None),
        P(),
    )
    return jax.shard_map(
        shards,
        mesh=mesh,
        in_specs=placed,
        out_specs=(P("freq", None, None, None), P("freq", None, None, None), P()),
        check_vma=False,
    )
```

```python
from functools import partial

import jax
import jax.numpy as jnp
import numpy as np
from jax import lax
from jax.experimental import pallas as pl
from jax.experimental.pallas import tpu as pltpu
from jax.sharding import PartitionSpec as P

ITERS = 2
RHO = 16.0
LANES = 128
OUTER = 4


def split(block):
    return ([block[i] for i in range(4)], [block[i + 4] for i in range(4)])


def product(left, right):
    lr, li = left
    rr, ri = right
    out_real, out_imag = [], []
    for row in range(2):
        for col in range(2):
            a, b = 2 * row, 2 * row + 1
            out_real.append(lr[a] * rr[col] - li[a] * ri[col] + lr[b] * rr[col + 2] - li[b] * ri[col + 2])
            out_imag.append(lr[a] * ri[col] + li[a] * rr[col] + lr[b] * ri[col + 2] + li[b] * rr[col + 2])
    return (out_real, out_imag)


def product_right_adjoint(left, right):
    lr, li = left
    rr, ri = right
    out_real, out_imag = [], []
    for row in range(2):
        for col in range(2):
            a, b, c, d = 2 * row, 2 * row + 1, 2 * col, 2 * col + 1
            out_real.append(lr[a] * rr[c] + li[a] * ri[c] + lr[b] * rr[d] + li[b] * ri[d])
            out_imag.append(li[a] * rr[c] - lr[a] * ri[c] + li[b] * rr[d] - lr[b] * ri[d])
    return (out_real, out_imag)


def product_left_adjoint(left, right):
    lr, li = left
    rr, ri = right
    out_real, out_imag = [], []
    for row in range(2):
        for col in range(2):
            a, b, c, d = row, row + 2, col, col + 2
            out_real.append(lr[a] * rr[c] + li[a] * ri[c] + lr[b] * rr[d] + li[b] * ri[d])
            out_imag.append(lr[a] * ri[c] - li[a] * rr[c] + lr[b] * ri[d] - li[b] * rr[d])
    return (out_real, out_imag)


def normal(r, i, rows):
    (a, b), (c, d) = rows
    top = r[a] * r[a] + i[a] * i[a] + r[b] * r[b] + i[b] * i[b]
    bottom = r[c] * r[c] + i[c] * i[c] + r[d] * r[d] + i[d] * i[d]
    real = r[a] * r[c] + i[a] * i[c] + r[b] * r[d] + i[b] * i[d]
    imag = i[a] * r[c] - r[a] * i[c] + i[b] * r[d] - r[b] * i[d]
    return top, bottom, real, imag


def basis_weights(count):
    x = (2.0 * np.arange(count, dtype=np.float64) + 1.0) / count - 1.0
    basis = np.stack([np.ones_like(x), x, 1.5 * x * x - 0.5, 2.5 * x * x * x - 1.5 * x], axis=1)
    return np.linalg.solve(basis.T @ basis, basis.T)


def halves(value):
    high = value.astype(jnp.bfloat16)
    return high, (value - high.astype(jnp.float32)).astype(jnp.bfloat16)


def from_basis(bases, f, coefficients):
    total = coefficients[0]
    for j in range(1, len(coefficients)):
        total = total + bases[f][j] * coefficients[j]
    return total


def local_bases(F, nf):
    bases = []
    for f in range(F):
        channel = (lax.axis_index("freq") * F + f).astype(jnp.float32)
        x = (2.0 * channel + 1.0) / (F * nf) - 1.0
        bases.append([None, x, 1.5 * x * x - 0.5, 2.5 * x * x * x - 1.5 * x])
    return bases


SOURCES = ((1, 3, 2), (0, 2, 3), (1, 0, 3), (2, 0, 1))
FIRST = (
    ((1, 0), (0, 1), (2, 0)),
    ((0, 0), (1, 1), (2, 0)),
    ((1, 0), (2, 1), (3, 0)),
    ((0, 0), (3, 1), (1, 0), (2, 0)),
)
AFTER = (((3, 0),), (), (), ())
RELAYS = (
    {1: ((0, 1),), 3: ((0, 1),)},
    {2: ((0, 0), (1, 1), (0, 1)), 0: ((1, 1),), 3: ((1, 1),)},
    {1: ((3, 0), (2, 1)), 0: ((2, 1),), 3: ((2, 1),)},
    {2: ((3, 1),), 0: ((3, 1),), 1: ((3, 1),)},
)


def spread(targets, inner):
    return [(row, e) for row, aside in targets for e in (range(1, inner) if aside else (0,))]


def targets_of(row, inner):
    near = set(spread(FIRST[row], inner))
    for found in RELAYS[row].values():
        near |= set(spread(found, inner))
    return near


def store_kernel(*refs):
    count = len(refs) // 2
    sem = refs[-1]
    copies = [pltpu.make_async_copy(refs[i], refs[count + i], sem.at[i]) for i in range(count)]
    for copy in copies:
        copy.start()
    for copy in copies:
        copy.wait()


def kernel(cfg, vis_hbm, coh_hbm, pairs_hbm, gains_hbm, duals_hbm, poly_hbm,
           gains_out, duals_out, poly_out,
           mixed, data, hot, tall, terms, early, jones, taken, pull, vis_ref, coh_ref, pairs_ref, gains_ref, duals_ref, poly_ref,
           tm_send, tm_recv, far, fq_send, fq_recv, load_sem):
    F, K, S, nt, nf, inner, chunks, terms_poly = cfg
    CH = S // chunks
    C = 8 * K
    tm = lax.axis_index("tm")
    fq = lax.axis_index("freq")
    z, y = tm // inner, tm % inner
    partner = fq + 1 - 2 * (fq % 2)
    MESH = pl.DeviceIdType.MESH
    columns_apart = range(1, inner)
    others = range(1, nf // 2)

    def role(act):
        for row in range(OUTER):
            pl.when(z == row)(lambda row=row: act(row))

    def chosen(table):
        found = table[0]
        for row in range(1, OUTER):
            found = jnp.where(z == row, table[row], found)
        return found

    nth = [chosen([SOURCES[row][k] for row in range(OUTER)]) for k in range(OUTER - 1)]

    def at(row, e):
        return row * inner + (y + e) % inner

    line = lambda k: (0, k)
    side = lambda k: (1, k)
    places = [("own", 0)]
    for group in ("mates", line(0), line(1), side(0), line(2), side(1), side(2)):
        places += [(group, e) for _, e in spread(((0, group == "mates" or group[0]),), inner)]
    blocks = [at(nth[group[1]] if isinstance(group, tuple) else z, e) for group, e in places]
    until = lambda group: [other for other, _ in places].index(group)

    def across(fq, d):
        there = (fq + 2 * d) % nf
        return there + 1 - 2 * (there % 2)

    barrier = pltpu.get_barrier_semaphore()

    def greet(peer):
        pl.semaphore_signal(barrier, inc=1, device_id=peer, device_id_type=MESH)

    def greet_rows(row):
        for other in range(OUTER):
            for there, e in sorted(targets_of(other, inner)):
                if there == row:
                    greet({"tm": at(other, inner - e)})

    role(greet_rows)
    greet({"freq": partner})
    for d in others:
        greet({"freq": across(fq, d)})

    loads = [pltpu.make_async_copy(src, dst, load_sem.at[i]) for i, (src, dst) in enumerate(
        ((coh_hbm, coh_ref), (vis_hbm, vis_ref), (pairs_hbm, pairs_ref),
         (gains_hbm, gains_ref), (duals_hbm, duals_ref), (poly_hbm, poly_ref)))]
    for load in loads:
        load.start()
    near = chosen([len(targets_of(row, inner)) for row in range(OUTER)])
    pl.semaphore_wait(barrier, near + 1 + (nf // 2 - 1))

    def greet_far(row):
        for other in range(OUTER):
            for there, _ in AFTER[other]:
                if there == row:
                    pl.semaphore_signal(far, inc=1, device_id={"tm": at(other, 0)}, device_id_type=MESH)

    role(greet_far)
    for load in loads[:3]:
        load.wait()
    data[tm, 0, 0:8, :] = jnp.zeros((8, LANES), jnp.float32)
    data[tm, 0, 0:2, :] = pairs_ref[...].astype(jnp.float32)
    for f in range(F):
        data[tm, f, 8:16, :] = vis_ref[f]
        data[tm, f, 16:, :] = coh_ref[f].astype(jnp.float32).reshape(C, LANES)

    def tm_copy(block, f, slot, device):
        rows = pl.ds(0, 16 + C) if f == 0 else pl.ds(8, 8 + C)
        return pltpu.make_async_remote_copy(
            src_ref=data.at[block, f, rows], dst_ref=data.at[block, f, rows],
            send_sem=tm_send.at[slot], recv_sem=tm_recv.at[block, f],
            device_id={"tm": device}, device_id_type=MESH)

    def arrived(block, f):
        tm_copy(block, f, 0, at(z, 1)).wait_recv()

    sends = []
    row_sends = [[] for _ in range(OUTER)]

    def send(row, source, f, targets):
        for there, e in spread(targets, inner):
            tm_copy(at(source, 0), f, len(row_sends[row]), at(there, e)).start()
            row_sends[row].append((source, f, there, e))

    def accept(group, f):
        def act(row):
            source, aside = (row, 1) if group == "mates" else (SOURCES[row][group[1]], group[0])
            for _, e in spread(((source, aside),), inner):
                arrived(at(source, e), f)
                if not aside:
                    send(row, source, f, relays(row, source, f))

        role(act)

    def relays(row, source, f):
        return RELAYS[row].get(source, ())

    stations = lax.broadcasted_iota(jnp.int32, (S, LANES), 0).astype(jnp.float32)

    across_stations = lax.broadcasted_iota(jnp.int32, (LANES, S), 1).astype(jnp.float32)

    def columns(place, half):
        return pl.ds((2 * place + half) * LANES, LANES)

    def make_hot(place):
        block = blocks[place]
        for half in range(2):
            row = data[block, 0, half : half + 1, :]
            hot[:, columns(place, half)] = jnp.where(stations == row, 1.0, 0.0).astype(jnp.bfloat16)
        turned = data[block, 0, 0:8, :].T
        for half in range(2):
            tall[columns(place, half), :] = jnp.where(across_stations == turned[:, half : half + 1], 1.0, 0.0).astype(jnp.bfloat16)

    def load_gains(gains, f):
        high, low = halves(gains[f].reshape(C, S))
        jones[2 * f * C : (2 * f + 1) * C, :] = high
        jones[(2 * f + 1) * C : (2 * f + 2) * C, :] = low

    def gather(place, first, last):
        both = pl.ds(place * 2 * LANES, 2 * LANES)
        found = jnp.dot(jones[2 * first * C : 2 * last * C, :], hot[:, both], preferred_element_type=jnp.float32)
        for f in range(first, last):
            base = 2 * (f - first) * C
            taken[place, f] = found[base : base + C] + found[base + C : base + 2 * C]

    def rows_sums(place, f):
        block = blocks[place]
        first = split([taken[place, f, c * K : (c + 1) * K, :LANES] for c in range(8)])
        second = split([taken[place, f, c * K : (c + 1) * K, LANES:] for c in range(8)])
        sky = split([data[block, f, 16 + c * K : 16 + (c + 1) * K, :] for c in range(8)])
        left = product(first, sky)
        right = product_right_adjoint(sky, second)
        model = product_right_adjoint(left, second)
        model = model[0] + model[1]
        residual = []
        for c in range(8):
            seen = data[block, f, 8 + c : 9 + c, :]
            residual.append(jnp.broadcast_to(seen - jnp.sum(model[c], axis=0, keepdims=True), (K, LANES)))
        residual = split(residual)
        ends = []
        out = product_right_adjoint(residual, right)
        ends.append(out[0] + out[1] + list(normal(right[0], right[1], ((0, 1), (2, 3)))))
        out = product_left_adjoint(residual, left)
        top, bottom, real, imag = normal(left[0], left[1], ((0, 2), (1, 3)))
        ends.append(out[0] + out[1] + [top, bottom, real, -imag])
        for half in range(2):
            high, low = halves(jnp.concatenate(ends[half], axis=0))
            terms[f, : 12 * K, columns(place, half)] = high
            terms[f, 12 * K :, columns(place, half)] = low

    bases = local_bases(F, nf)

    def pulls(f):
        for c in range(8):
            prior = from_basis(bases, f, [poly_ref[j, c] for j in range(terms_poly)])
            pull[f, c] = RHO * prior - duals_ref[f, c]

    def scattered(f, places, lanes):
        some = slice(places[0] * 2 * LANES, places[1] * 2 * LANES)
        sums = jnp.dot(terms[f, :, some], tall[some, lanes], preferred_element_type=jnp.float32)
        return sums[: 12 * K] + sums[12 * K :]

    def update(source, f, damping, chunk, done):
        lanes = slice(chunk * CH, (chunk + 1) * CH)
        sums = scattered(f, (done, nt), lanes)
        if done:
            sums = sums + early[f, :, lanes]
        part = [sums[c * K : (c + 1) * K] for c in range(12)]
        old, step = [], []
        for c in range(8):
            gain = source[f, c, :, lanes]
            old.append(gain)
            step.append(part[c] + pull[f, c, :, lanes] - RHO * gain)
        top, bottom, real, imag = part[8:]
        shift = damping * 0.5 * (top + bottom) + RHO
        upper, lower = top + shift, bottom + shift
        scale = 1.0 / (upper * lower - real * real - imag * imag)
        a, d, br, bi = lower * scale, upper * scale, -real * scale, -imag * scale
        sr, si = split(step)
        for row in range(2):
            p, q = 2 * row, 2 * row + 1
            gains_out[f, p, :, lanes] = old[p] + sr[p] * a + sr[q] * br + si[q] * bi
            gains_out[f, p + 4, :, lanes] = old[p + 4] + si[p] * a + si[q] * br - sr[q] * bi
            gains_out[f, q, :, lanes] = old[q] + sr[p] * br - si[p] * bi + sr[q] * d
            gains_out[f, q + 4, :, lanes] = old[q + 4] + si[p] * br + sr[p] * bi + si[q] * d

    def take(place, f):
        if f == 0:
            make_hot(place)
            gather(place, 0, F)
        rows_sums(place, f)

    def fq_copy(owner, f, chunk, slot, device):
        return pltpu.make_async_remote_copy(
            src_ref=mixed.at[owner, f, chunk], dst_ref=mixed.at[owner, f, chunk],
            send_sem=fq_send.at[slot, f, chunk], recv_sem=fq_recv.at[owner, f, chunk],
            device_id={"freq": device}, device_id_type=MESH)

    def fq_start(owner, f, chunk, slot, device):
        copy = fq_copy(owner, f, chunk, slot, device)
        copy.start()
        sends.append(copy)

    def sum_early(f, done):
        early[f] = scattered(f, (0, done), slice(0, S))

    def finish(f, done):
        for chunk in range(chunks):
            update(gains_ref, f, 12.0, chunk, done)
        for step in range(1, ITERS):
            load_gains(gains_out, f)

            for place in range(nt):
                gather(place, f, f + 1)
            for place in range(nt):
                rows_sums(place, f)

            for chunk in range(chunks):
                update(gains_out, f, 12.0 * 0.5**step, chunk, 0)
                if step == ITERS - 1:
                    lanes = slice(chunk * CH, (chunk + 1) * CH)
                    value = gains_out[f, :, :, lanes] + duals_ref[f, :, :, lanes] * (1.0 / RHO)
                    mixed[fq, f, chunk] = value.reshape(C, CH)
                    for d in others:
                        fq_start(fq, f, chunk, d, across(fq, d))
                    fq_start(fq, f, chunk, 0, partner)

    def forward(f):
        for chunk in range(chunks):
            for d in others:
                owner = across(fq, nf // 2 - d)
                fq_copy(owner, f, chunk, 0, partner).wait_recv()
                fq_start(owner, f, chunk, nf // 2 + d, partner)

    weights = basis_weights(F * nf)

    def received(f, chunk):
        fq_copy(partner, f, chunk, 0, partner).wait_recv()
        for d in others:
            fq_copy(across(partner, nf // 2 - d), f, chunk, 0, partner).wait_recv()

    def fit(f, chunk):
        lanes = slice(chunk * CH, (chunk + 1) * CH)
        for c in range(8):
            values = [mixed[n, f, chunk, c * K : (c + 1) * K, :] for n in range(nf)]
            coefficients = []
            for j in range(terms_poly):
                total = float(weights[j, f]) * values[0]
                for n in range(1, nf):
                    total = total + float(weights[j, n * F + f]) * values[n]
                if f > 0:
                    total = total + poly_out[j, c, :, lanes]
                poly_out[j, c, :, lanes] = total
                coefficients.append(total)
            if f == F - 1:
                for g in range(F):
                    prior = from_basis(bases, g, coefficients)
                    duals_out[g, c, :, lanes] = duals_ref[g, c, :, lanes] + RHO * (gains_out[g, c, :, lanes] - prior)

    later = range(1, F)
    def send_first(row):
        for f in range(F):
            send(row, row, f, FIRST[row])

    role(send_first)

    loads[3].wait()
    for f in range(F):
        load_gains(gains_ref, f)
    for f in range(F):
        take(0, f)

    def send_after(row):
        if AFTER[row]:
            pl.semaphore_wait(far, len(AFTER[row]))
            for f in range(F):
                send(row, row, f, AFTER[row])

    role(send_after)
    loads[4].wait()
    loads[5].wait()
    for f in range(F):
        pulls(f)

    arrivals = [("mates", 0), (line(0), 0), (line(1), 0)]
    for f in later:
        arrivals += [("mates", f), (line(0), f), (line(1), f)]
    arrivals += [(side(0), 0), (line(2), 0)]
    for f in later:
        arrivals += [(line(2), f)]
    arrivals += [(side(1), 0)]
    for f in later:
        arrivals += [(side(0), f)]
    arrivals += [(side(2), 0)]
    for f in later:
        arrivals += [(side(1), f), (side(2), f)]

    def have(group, f):
        while (group, f) in arrivals:
            accept(*arrivals.pop(0))
        for place, (other, _) in enumerate(places):
            if other == group:
                take(place, f)

    have("mates", 0)
    have(line(0), 0)
    have(line(1), 0)
    for f in later:
        have("mates", f)
        have(line(0), f)
        have(line(1), f)
    have(side(0), 0)
    have(line(2), 0)
    have(side(1), 0)
    for f in later:
        have(line(2), f)
        have(side(0), f)
    sum_early(0, until(side(2)))
    for f in later:
        sum_early(f, until(side(1)))
    have(side(2), 0)
    finish(0, until(side(2)))
    for f in later:
        have(side(1), f)
        have(side(2), f)
        finish(f, until(side(1)))
        forward(f - 1)
        for chunk in range(chunks):
            received(f - 1, chunk)
            fit(f - 1, chunk)
    forward(F - 1)
    for chunk in range(chunks):
        received(F - 1, chunk)
        fit(F - 1, chunk)
    for copy in sends:
        copy.wait_send()

    def drain(row):
        for slot, (source, f, there, e) in enumerate(row_sends[row]):
            tm_copy(at(source, 0), f, slot, at(there, e)).wait_send()

    role(drain)


def solution(mesh):
    nt, nf = mesh.shape["tm"], mesh.shape["freq"]

    def shards(*operands):
        visibilities, coherencies, pairs, gains_start, _, poly_start = operands
        F, _, K, S = gains_start.shape
        inner = nt // OUTER
        chunks = 2
        C = 8 * K
        CH = S // chunks
        cfg = (F, K, S, nt, nf, inner, chunks, poly_start.shape[0])
        wide = lambda x: pltpu.VMEM(x.shape, jnp.float32)
        vmem = pl.BlockSpec(memory_space=pltpu.VMEM)
        hbm = pl.BlockSpec(memory_space=pltpu.HBM)
        results = (gains_start, gains_start, poly_start)
        shapes = tuple(jax.ShapeDtypeStruct(x.shape, jnp.float32) for x in results)
        held = pl.pallas_call(
            partial(kernel, cfg),
            out_shape=shapes,
            in_specs=[hbm] * 6,
            out_specs=(vmem,) * 3,
            scratch_shapes=[
                pltpu.VMEM((nf, F, chunks, C, CH), jnp.float32),
                pltpu.VMEM((nt, F, 16 + C, LANES), jnp.float32),
                pltpu.VMEM((S, nt * 2 * LANES), jnp.bfloat16),
                pltpu.VMEM((nt * 2 * LANES, S), jnp.bfloat16),
                pltpu.VMEM((F, 2 * 12 * K, nt * 2 * LANES), jnp.bfloat16),
                pltpu.VMEM((F, 12 * K, S), jnp.float32),
                pltpu.VMEM((2 * F * C, S), jnp.bfloat16),
                pltpu.VMEM((nt, F, C, 2 * LANES), jnp.float32),
                wide(gains_start),
                pltpu.VMEM(visibilities.shape, jnp.float32),
                pltpu.VMEM(coherencies.shape, jnp.bfloat16),
                pltpu.VMEM(pairs.shape, jnp.int32),
                wide(gains_start),
                wide(gains_start),
                wide(poly_start),
                pltpu.SemaphoreType.DMA((2 * OUTER * inner * F,)),
                pltpu.SemaphoreType.DMA((nt, F)),
                pltpu.SemaphoreType.REGULAR,
                pltpu.SemaphoreType.DMA((nf + 1, F, chunks)),
                pltpu.SemaphoreType.DMA((nf, F, chunks)),
                pltpu.SemaphoreType.DMA((6,)),
            ],
            compiler_params=pltpu.CompilerParams(collective_id=0, has_side_effects=True,
                                                 vmem_limit_bytes=40 * 2**20),
        )(*(pltpu.with_memory_space_constraint(x, pltpu.HBM) for x in operands))
        return pl.pallas_call(
            store_kernel,
            out_shape=shapes,
            in_specs=[vmem] * 3,
            out_specs=(hbm,) * 3,
            scratch_shapes=[pltpu.SemaphoreType.DMA((3,))],
            compiler_params=pltpu.CompilerParams(vmem_limit_bytes=16 * 2**20),
        )(*held)

    placed = (
        P("freq", None, "tm"),
        P("freq", None, None, "tm"),
        P(None, "tm"),
        P("freq", None, None, None),
        P("freq", None, None, None),
        P(),
    )
    return jax.shard_map(
        shards,
        mesh=mesh,
        in_specs=placed,
        out_specs=(P("freq", None, None, None), P("freq", None, None, None), P()),
        check_vma=False,
    )
```

```python
from functools import partial

import jax
import jax.numpy as jnp
import numpy as np
from jax import lax
from jax.experimental import pallas as pl
from jax.experimental.pallas import tpu as pltpu
from jax.sharding import PartitionSpec as P

ITERS = 2
RHO = 16.0
LANES = 128
OUTER = 4


def split(block):
    return ([block[i] for i in range(4)], [block[i + 4] for i in range(4)])


def product(left, right):
    lr, li = left
    rr, ri = right
    out_real, out_imag = [], []
    for row in range(2):
        for col in range(2):
            a, b = 2 * row, 2 * row + 1
            out_real.append(lr[a] * rr[col] - li[a] * ri[col] + lr[b] * rr[col + 2] - li[b] * ri[col + 2])
            out_imag.append(lr[a] * ri[col] + li[a] * rr[col] + lr[b] * ri[col + 2] + li[b] * rr[col + 2])
    return (out_real, out_imag)


def product_right_adjoint(left, right):
    lr, li = left
    rr, ri = right
    out_real, out_imag = [], []
    for row in range(2):
        for col in range(2):
            a, b, c, d = 2 * row, 2 * row + 1, 2 * col, 2 * col + 1
            out_real.append(lr[a] * rr[c] + li[a] * ri[c] + lr[b] * rr[d] + li[b] * ri[d])
            out_imag.append(li[a] * rr[c] - lr[a] * ri[c] + li[b] * rr[d] - lr[b] * ri[d])
    return (out_real, out_imag)


def product_left_adjoint(left, right):
    lr, li = left
    rr, ri = right
    out_real, out_imag = [], []
    for row in range(2):
        for col in range(2):
            a, b, c, d = row, row + 2, col, col + 2
            out_real.append(lr[a] * rr[c] + li[a] * ri[c] + lr[b] * rr[d] + li[b] * ri[d])
            out_imag.append(lr[a] * ri[c] - li[a] * rr[c] + lr[b] * ri[d] - li[b] * rr[d])
    return (out_real, out_imag)


def normal(r, i, rows):
    (a, b), (c, d) = rows
    top = r[a] * r[a] + i[a] * i[a] + r[b] * r[b] + i[b] * i[b]
    bottom = r[c] * r[c] + i[c] * i[c] + r[d] * r[d] + i[d] * i[d]
    real = r[a] * r[c] + i[a] * i[c] + r[b] * r[d] + i[b] * i[d]
    imag = i[a] * r[c] - r[a] * i[c] + i[b] * r[d] - r[b] * i[d]
    return top, bottom, real, imag


def basis_weights(count):
    x = (2.0 * np.arange(count, dtype=np.float64) + 1.0) / count - 1.0
    basis = np.stack([np.ones_like(x), x, 1.5 * x * x - 0.5, 2.5 * x * x * x - 1.5 * x], axis=1)
    return np.linalg.solve(basis.T @ basis, basis.T)


def halves(value):
    high = value.astype(jnp.bfloat16)
    return high, (value - high.astype(jnp.float32)).astype(jnp.bfloat16)


def from_basis(bases, f, coefficients):
    total = coefficients[0]
    for j in range(1, len(coefficients)):
        total = total + bases[f][j] * coefficients[j]
    return total


def local_bases(F, nf):
    bases = []
    for f in range(F):
        channel = (lax.axis_index("freq") * F + f).astype(jnp.float32)
        x = (2.0 * channel + 1.0) / (F * nf) - 1.0
        bases.append([None, x, 1.5 * x * x - 0.5, 2.5 * x * x * x - 1.5 * x])
    return bases


SOURCES = ((1, 3, 2), (0, 2, 3), (1, 0, 3), (2, 0, 1))
FIRST = (
    ((1, 0), (0, 1), (2, 0)),
    ((0, 0), (1, 1), (2, 0)),
    ((1, 0), (2, 1), (3, 0)),
    ((0, 0), (3, 1), (1, 0), (2, 0)),
)
AFTER = (((3, 0),), (), (), ())
RELAYS = (
    {1: ((0, 1),), 3: ((0, 1),)},
    {2: ((0, 0), (1, 1), (0, 1)), 0: ((1, 1),), 3: ((1, 1),)},
    {1: ((3, 0), (2, 1)), 0: ((2, 1),), 3: ((2, 1),)},
    {2: ((3, 1),), 0: ((3, 1),), 1: ((3, 1),)},
)


def spread(targets, inner):
    return [(row, e) for row, aside in targets for e in (range(1, inner) if aside else (0,))]


def targets_of(row, inner):
    near = set(spread(FIRST[row], inner))
    for found in RELAYS[row].values():
        near |= set(spread(found, inner))
    return near


def store_kernel(*refs):
    count = len(refs) // 2
    sem = refs[-1]
    copies = [pltpu.make_async_copy(refs[i], refs[count + i], sem.at[i]) for i in range(count)]
    for copy in copies:
        copy.start()
    for copy in copies:
        copy.wait()


def kernel(cfg, vis_hbm, coh_hbm, pairs_hbm, gains_hbm, duals_hbm, poly_hbm,
           gains_out, duals_out, poly_out,
           mixed, data, hot, tall, terms, early, jones, taken, pull, vis_ref, coh_ref, pairs_ref, gains_ref, duals_ref, poly_ref,
           tm_send, tm_recv, far, fq_send, fq_recv, load_sem):
    F, K, S, nt, nf, inner, chunks, terms_poly = cfg
    CH = S // chunks
    C = 8 * K
    tm = lax.axis_index("tm")
    fq = lax.axis_index("freq")
    z, y = tm // inner, tm % inner
    partner = fq + 1 - 2 * (fq % 2)
    MESH = pl.DeviceIdType.MESH
    columns_apart = range(1, inner)
    others = range(1, nf // 2)

    def role(act):
        for row in range(OUTER):
            pl.when(z == row)(lambda row=row: act(row))

    def chosen(table):
        found = table[0]
        for row in range(1, OUTER):
            found = jnp.where(z == row, table[row], found)
        return found

    nth = [chosen([SOURCES[row][k] for row in range(OUTER)]) for k in range(OUTER - 1)]

    def at(row, e):
        return row * inner + (y + e) % inner

    line = lambda k: (0, k)
    side = lambda k: (1, k)
    places = [("own", 0)]
    for group in ("mates", line(0), line(1), side(0), line(2), side(1), side(2)):
        places += [(group, e) for _, e in spread(((0, group == "mates" or group[0]),), inner)]
    blocks = [at(nth[group[1]] if isinstance(group, tuple) else z, e) for group, e in places]
    until = lambda group: [other for other, _ in places].index(group)

    def across(fq, d):
        there = (fq + 2 * d) % nf
        return there + 1 - 2 * (there % 2)

    barrier = pltpu.get_barrier_semaphore()

    def greet(peer):
        pl.semaphore_signal(barrier, inc=1, device_id=peer, device_id_type=MESH)

    def greet_rows(row):
        for other in range(OUTER):
            for there, e in sorted(targets_of(other, inner)):
                if there == row:
                    greet({"tm": at(other, inner - e)})

    role(greet_rows)
    greet({"freq": partner})
    for d in others:
        greet({"freq": across(fq, d)})

    loads = [pltpu.make_async_copy(src, dst, load_sem.at[i]) for i, (src, dst) in enumerate(
        ((coh_hbm, coh_ref), (vis_hbm, vis_ref), (pairs_hbm, pairs_ref),
         (gains_hbm, gains_ref), (duals_hbm, duals_ref), (poly_hbm, poly_ref)))]
    for load in loads:
        load.start()
    near = chosen([len(targets_of(row, inner)) for row in range(OUTER)])
    pl.semaphore_wait(barrier, near + 1 + (nf // 2 - 1))

    def greet_far(row):
        for other in range(OUTER):
            for there, _ in AFTER[other]:
                if there == row:
                    pl.semaphore_signal(far, inc=1, device_id={"tm": at(other, 0)}, device_id_type=MESH)

    role(greet_far)
    for load in loads[:3]:
        load.wait()
    data[tm, 0, 0:8, :] = jnp.zeros((8, LANES), jnp.float32)
    data[tm, 0, 0:2, :] = pairs_ref[...].astype(jnp.float32)
    for f in range(F):
        data[tm, f, 8:16, :] = vis_ref[f]
        data[tm, f, 16:, :] = coh_ref[f].astype(jnp.float32).reshape(C, LANES)

    def tm_copy(block, f, slot, device):
        rows = pl.ds(0, 16 + C) if f == 0 else pl.ds(8, 8 + C)
        return pltpu.make_async_remote_copy(
            src_ref=data.at[block, f, rows], dst_ref=data.at[block, f, rows],
            send_sem=tm_send.at[slot], recv_sem=tm_recv.at[block, f],
            device_id={"tm": device}, device_id_type=MESH)

    def arrived(block, f):
        tm_copy(block, f, 0, at(z, 1)).wait_recv()

    sends = []
    row_sends = [[] for _ in range(OUTER)]

    def send(row, source, f, targets):
        for there, e in spread(targets, inner):
            tm_copy(at(source, 0), f, len(row_sends[row]), at(there, e)).start()
            row_sends[row].append((source, f, there, e))

    def accept(group, f):
        def act(row):
            source, aside = (row, 1) if group == "mates" else (SOURCES[row][group[1]], group[0])
            for _, e in spread(((source, aside),), inner):
                arrived(at(source, e), f)
                if not aside:
                    send(row, source, f, relays(row, source, f))

        role(act)

    def relays(row, source, f):
        return RELAYS[row].get(source, ())

    stations = lax.broadcasted_iota(jnp.int32, (S, LANES), 0).astype(jnp.float32)

    across_stations = lax.broadcasted_iota(jnp.int32, (LANES, S), 1).astype(jnp.float32)

    def columns(place, half):
        return pl.ds((2 * place + half) * LANES, LANES)

    def make_hot(place):
        block = blocks[place]
        for half in range(2):
            row = data[block, 0, half : half + 1, :]
            hot[:, columns(place, half)] = jnp.where(stations == row, 1.0, 0.0).astype(jnp.bfloat16)
        turned = data[block, 0, 0:8, :].T
        for half in range(2):
            tall[columns(place, half), :] = jnp.where(across_stations == turned[:, half : half + 1], 1.0, 0.0).astype(jnp.bfloat16)

    def load_gains(gains, f):
        high, low = halves(gains[f].reshape(C, S))
        jones[2 * f * C : (2 * f + 1) * C, :] = high
        jones[(2 * f + 1) * C : (2 * f + 2) * C, :] = low

    def gather(place, first, last):
        both = pl.ds(place * 2 * LANES, 2 * LANES)
        found = jnp.dot(jones[2 * first * C : 2 * last * C, :], hot[:, both], preferred_element_type=jnp.float32)
        for f in range(first, last):
            base = 2 * (f - first) * C
            taken[place, f] = found[base : base + C] + found[base + C : base + 2 * C]

    def rows_sums(place, f):
        block = blocks[place]
        first = split([taken[place, f, c * K : (c + 1) * K, :LANES] for c in range(8)])
        second = split([taken[place, f, c * K : (c + 1) * K, LANES:] for c in range(8)])
        sky = split([data[block, f, 16 + c * K : 16 + (c + 1) * K, :] for c in range(8)])
        left = product(first, sky)
        right = product_right_adjoint(sky, second)
        model = product_right_adjoint(left, second)
        model = model[0] + model[1]
        residual = []
        for c in range(8):
            seen = data[block, f, 8 + c : 9 + c, :]
            residual.append(jnp.broadcast_to(seen - jnp.sum(model[c], axis=0, keepdims=True), (K, LANES)))
        residual = split(residual)
        ends = []
        out = product_right_adjoint(residual, right)
        ends.append(out[0] + out[1] + list(normal(right[0], right[1], ((0, 1), (2, 3)))))
        out = product_left_adjoint(residual, left)
        top, bottom, real, imag = normal(left[0], left[1], ((0, 2), (1, 3)))
        ends.append(out[0] + out[1] + [top, bottom, real, -imag])
        for half in range(2):
            high, low = halves(jnp.concatenate(ends[half], axis=0))
            terms[f, : 12 * K, columns(place, half)] = high
            terms[f, 12 * K :, columns(place, half)] = low

    bases = local_bases(F, nf)

    def pulls(f):
        for c in range(8):
            prior = from_basis(bases, f, [poly_ref[j, c] for j in range(terms_poly)])
            pull[f, c] = RHO * prior - duals_ref[f, c]

    def scattered(f, places, lanes):
        some = slice(places[0] * 2 * LANES, places[1] * 2 * LANES)
        sums = jnp.dot(terms[f, :, some], tall[some, lanes], preferred_element_type=jnp.float32)
        return sums[: 12 * K] + sums[12 * K :]

    def update(source, f, damping, chunk, done):
        lanes = slice(chunk * CH, (chunk + 1) * CH)
        sums = scattered(f, (done, nt), lanes)
        if done:
            sums = sums + early[f, :, lanes]
        part = [sums[c * K : (c + 1) * K] for c in range(12)]
        old, step = [], []
        for c in range(8):
            gain = source[f, c, :, lanes]
            old.append(gain)
            step.append(part[c] + pull[f, c, :, lanes] - RHO * gain)
        top, bottom, real, imag = part[8:]
        shift = damping * 0.5 * (top + bottom) + RHO
        upper, lower = top + shift, bottom + shift
        scale = 1.0 / (upper * lower - real * real - imag * imag)
        a, d, br, bi = lower * scale, upper * scale, -real * scale, -imag * scale
        sr, si = split(step)
        for row in range(2):
            p, q = 2 * row, 2 * row + 1
            gains_out[f, p, :, lanes] = old[p] + sr[p] * a + sr[q] * br + si[q] * bi
            gains_out[f, p + 4, :, lanes] = old[p + 4] + si[p] * a + si[q] * br - sr[q] * bi
            gains_out[f, q, :, lanes] = old[q] + sr[p] * br - si[p] * bi + sr[q] * d
            gains_out[f, q + 4, :, lanes] = old[q + 4] + si[p] * br + sr[p] * bi + si[q] * d

    def take(place, f):
        if f == 0:
            make_hot(place)
            gather(place, 0, F)
        rows_sums(place, f)

    def fq_copy(owner, f, chunk, slot, device):
        return pltpu.make_async_remote_copy(
            src_ref=mixed.at[owner, f, chunk], dst_ref=mixed.at[owner, f, chunk],
            send_sem=fq_send.at[slot, f, chunk], recv_sem=fq_recv.at[owner, f, chunk],
            device_id={"freq": device}, device_id_type=MESH)

    def fq_start(owner, f, chunk, slot, device):
        copy = fq_copy(owner, f, chunk, slot, device)
        copy.start()
        sends.append(copy)

    def sum_early(f, done):
        early[f] = scattered(f, (0, done), slice(0, S))

    def finish(f, done):
        for chunk in range(chunks):
            update(gains_ref, f, 12.0, chunk, done)
        for step in range(1, ITERS):
            load_gains(gains_out, f)

            for place in range(nt):
                gather(place, f, f + 1)
            for place in range(nt):
                rows_sums(place, f)

            for chunk in range(chunks):
                update(gains_out, f, 12.0 * 0.5**step, chunk, 0)
                if step == ITERS - 1:
                    lanes = slice(chunk * CH, (chunk + 1) * CH)
                    value = gains_out[f, :, :, lanes] + duals_ref[f, :, :, lanes] * (1.0 / RHO)
                    mixed[fq, f, chunk] = value.reshape(C, CH)
                    for d in others:
                        fq_start(fq, f, chunk, d, across(fq, d))
                    fq_start(fq, f, chunk, 0, partner)

    def forward(f):
        for chunk in range(chunks):
            for d in others:
                owner = across(fq, nf // 2 - d)
                fq_copy(owner, f, chunk, 0, partner).wait_recv()
                fq_start(owner, f, chunk, nf // 2 + d, partner)

    weights = basis_weights(F * nf)

    def received(f, chunk):
        fq_copy(partner, f, chunk, 0, partner).wait_recv()
        for d in others:
            fq_copy(across(partner, nf // 2 - d), f, chunk, 0, partner).wait_recv()

    def fit(f, chunk):
        lanes = slice(chunk * CH, (chunk + 1) * CH)
        for c in range(8):
            values = [mixed[n, f, chunk, c * K : (c + 1) * K, :] for n in range(nf)]
            coefficients = []
            for j in range(terms_poly):
                total = float(weights[j, f]) * values[0]
                for n in range(1, nf):
                    total = total + float(weights[j, n * F + f]) * values[n]
                if f > 0:
                    total = total + poly_out[j, c, :, lanes]
                poly_out[j, c, :, lanes] = total
                coefficients.append(total)
            if f == F - 1:
                for g in range(F):
                    prior = from_basis(bases, g, coefficients)
                    duals_out[g, c, :, lanes] = duals_ref[g, c, :, lanes] + RHO * (gains_out[g, c, :, lanes] - prior)

    later = range(1, F)
    def send_first(row):
        for f in range(F):
            send(row, row, f, FIRST[row])

    role(send_first)

    loads[3].wait()
    for f in range(F):
        load_gains(gains_ref, f)
    for f in range(F):
        take(0, f)

    def send_after(row):
        if AFTER[row]:
            pl.semaphore_wait(far, len(AFTER[row]))
            for f in range(F):
                send(row, row, f, AFTER[row])

    role(send_after)
    loads[4].wait()
    loads[5].wait()
    for f in range(F):
        pulls(f)

    arrivals = [("mates", 0), (line(0), 0), (line(1), 0)]
    for f in later:
        arrivals += [("mates", f), (line(0), f), (line(1), f)]
    arrivals += [(side(0), 0), (line(2), 0)]
    for f in later:
        arrivals += [(line(2), f)]
    arrivals += [(side(1), 0)]
    for f in later:
        arrivals += [(side(0), f)]
    arrivals += [(side(2), 0)]
    for f in later:
        arrivals += [(side(1), f), (side(2), f)]

    def have(group, f):
        while (group, f) in arrivals:
            accept(*arrivals.pop(0))
        for place, (other, _) in enumerate(places):
            if other == group:
                take(place, f)

    have("mates", 0)
    have(line(0), 0)
    have(line(1), 0)
    for f in later:
        have("mates", f)
        have(line(0), f)
        have(line(1), f)
    have(side(0), 0)
    have(line(2), 0)
    have(side(1), 0)
    for f in later:
        have(line(2), f)
        have(side(0), f)
    sum_early(0, until(side(2)))
    for f in later:
        sum_early(f, until(side(1)))
    have(side(2), 0)
    finish(0, until(side(2)))
    for f in later:
        have(side(1), f)
        have(side(2), f)
        finish(f, until(side(1)))
        forward(f - 1)
        for chunk in range(chunks):
            received(f - 1, chunk)
            fit(f - 1, chunk)
    forward(F - 1)
    for chunk in range(chunks):
        received(F - 1, chunk)
        fit(F - 1, chunk)
    for copy in sends:
        copy.wait_send()

    def drain(row):
        for slot, (source, f, there, e) in enumerate(row_sends[row]):
            tm_copy(at(source, 0), f, slot, at(there, e)).wait_send()

    role(drain)


def solution(mesh):
    nt, nf = mesh.shape["tm"], mesh.shape["freq"]

    def shards(*operands):
        visibilities, coherencies, pairs, gains_start, _, poly_start = operands
        F, _, K, S = gains_start.shape
        inner = nt // OUTER
        chunks = 1
        C = 8 * K
        CH = S // chunks
        cfg = (F, K, S, nt, nf, inner, chunks, poly_start.shape[0])
        wide = lambda x: pltpu.VMEM(x.shape, jnp.float32)
        vmem = pl.BlockSpec(memory_space=pltpu.VMEM)
        hbm = pl.BlockSpec(memory_space=pltpu.HBM)
        results = (gains_start, gains_start, poly_start)
        shapes = tuple(jax.ShapeDtypeStruct(x.shape, jnp.float32) for x in results)
        held = pl.pallas_call(
            partial(kernel, cfg),
            out_shape=shapes,
            in_specs=[hbm] * 6,
            out_specs=(vmem,) * 3,
            scratch_shapes=[
                pltpu.VMEM((nf, F, chunks, C, CH), jnp.float32),
                pltpu.VMEM((nt, F, 16 + C, LANES), jnp.float32),
                pltpu.VMEM((S, nt * 2 * LANES), jnp.bfloat16),
                pltpu.VMEM((nt * 2 * LANES, S), jnp.bfloat16),
                pltpu.VMEM((F, 2 * 12 * K, nt * 2 * LANES), jnp.bfloat16),
                pltpu.VMEM((F, 12 * K, S), jnp.float32),
                pltpu.VMEM((2 * F * C, S), jnp.bfloat16),
                pltpu.VMEM((nt, F, C, 2 * LANES), jnp.float32),
                wide(gains_start),
                pltpu.VMEM(visibilities.shape, jnp.float32),
                pltpu.VMEM(coherencies.shape, jnp.bfloat16),
                pltpu.VMEM(pairs.shape, jnp.int32),
                wide(gains_start),
                wide(gains_start),
                wide(poly_start),
                pltpu.SemaphoreType.DMA((2 * OUTER * inner * F,)),
                pltpu.SemaphoreType.DMA((nt, F)),
                pltpu.SemaphoreType.REGULAR,
                pltpu.SemaphoreType.DMA((nf + 1, F, chunks)),
                pltpu.SemaphoreType.DMA((nf, F, chunks)),
                pltpu.SemaphoreType.DMA((6,)),
            ],
            compiler_params=pltpu.CompilerParams(collective_id=0, has_side_effects=True,
                                                 vmem_limit_bytes=40 * 2**20),
        )(*(pltpu.with_memory_space_constraint(x, pltpu.HBM) for x in operands))
        return pl.pallas_call(
            store_kernel,
            out_shape=shapes,
            in_specs=[vmem] * 3,
            out_specs=(hbm,) * 3,
            scratch_shapes=[pltpu.SemaphoreType.DMA((3,))],
            compiler_params=pltpu.CompilerParams(vmem_limit_bytes=16 * 2**20),
        )(*held)

    placed = (
        P("freq", None, "tm"),
        P("freq", None, None, "tm"),
        P(None, "tm"),
        P("freq", None, None, None),
        P("freq", None, None, None),
        P(),
    )
    return jax.shard_map(
        shards,
        mesh=mesh,
        in_specs=placed,
        out_specs=(P("freq", None, None, None), P("freq", None, None, None), P()),
        check_vma=False,
    )
```

```python
from functools import partial

import jax
import jax.numpy as jnp
import numpy as np
from jax import lax
from jax.experimental import pallas as pl
from jax.experimental.pallas import tpu as pltpu
from jax.sharding import PartitionSpec as P

ITERS = 2
RHO = 16.0
LANES = 128
OUTER = 4


def split(block):
    return ([block[i] for i in range(4)], [block[i + 4] for i in range(4)])


def product(left, right):
    lr, li = left
    rr, ri = right
    out_real, out_imag = [], []
    for row in range(2):
        for col in range(2):
            a, b = 2 * row, 2 * row + 1
            out_real.append(lr[a] * rr[col] - li[a] * ri[col] + lr[b] * rr[col + 2] - li[b] * ri[col + 2])
            out_imag.append(lr[a] * ri[col] + li[a] * rr[col] + lr[b] * ri[col + 2] + li[b] * rr[col + 2])
    return (out_real, out_imag)


def product_right_adjoint(left, right):
    lr, li = left
    rr, ri = right
    out_real, out_imag = [], []
    for row in range(2):
        for col in range(2):
            a, b, c, d = 2 * row, 2 * row + 1, 2 * col, 2 * col + 1
            out_real.append(lr[a] * rr[c] + li[a] * ri[c] + lr[b] * rr[d] + li[b] * ri[d])
            out_imag.append(li[a] * rr[c] - lr[a] * ri[c] + li[b] * rr[d] - lr[b] * ri[d])
    return (out_real, out_imag)


def product_left_adjoint(left, right):
    lr, li = left
    rr, ri = right
    out_real, out_imag = [], []
    for row in range(2):
        for col in range(2):
            a, b, c, d = row, row + 2, col, col + 2
            out_real.append(lr[a] * rr[c] + li[a] * ri[c] + lr[b] * rr[d] + li[b] * ri[d])
            out_imag.append(lr[a] * ri[c] - li[a] * rr[c] + lr[b] * ri[d] - li[b] * rr[d])
    return (out_real, out_imag)


def normal(r, i, rows):
    (a, b), (c, d) = rows
    top = r[a] * r[a] + i[a] * i[a] + r[b] * r[b] + i[b] * i[b]
    bottom = r[c] * r[c] + i[c] * i[c] + r[d] * r[d] + i[d] * i[d]
    real = r[a] * r[c] + i[a] * i[c] + r[b] * r[d] + i[b] * i[d]
    imag = i[a] * r[c] - r[a] * i[c] + i[b] * r[d] - r[b] * i[d]
    return top, bottom, real, imag


def basis_weights(count):
    x = (2.0 * np.arange(count, dtype=np.float64) + 1.0) / count - 1.0
    basis = np.stack([np.ones_like(x), x, 1.5 * x * x - 0.5, 2.5 * x * x * x - 1.5 * x], axis=1)
    return np.linalg.solve(basis.T @ basis, basis.T)


def halves(value):
    high = value.astype(jnp.bfloat16)
    return high, (value - high.astype(jnp.float32)).astype(jnp.bfloat16)


def from_basis(bases, f, coefficients):
    total = coefficients[0]
    for j in range(1, len(coefficients)):
        total = total + bases[f][j] * coefficients[j]
    return total


def local_bases(F, nf):
    bases = []
    for f in range(F):
        channel = (lax.axis_index("freq") * F + f).astype(jnp.float32)
        x = (2.0 * channel + 1.0) / (F * nf) - 1.0
        bases.append([None, x, 1.5 * x * x - 0.5, 2.5 * x * x * x - 1.5 * x])
    return bases


SOURCES = ((1, 3, 2), (0, 2, 3), (1, 0, 3), (2, 0, 1))
FIRST = (
    ((1, 0), (0, 1), (2, 0)),
    ((0, 0), (1, 1), (2, 0)),
    ((1, 0), (2, 1), (3, 0)),
    ((0, 0), (3, 1), (1, 0), (2, 0)),
)
AFTER = (((3, 0),), (), (), ())
RELAYS = (
    {1: ((0, 1),), 3: ((0, 1),)},
    {2: ((0, 0), (1, 1), (0, 1)), 0: ((1, 1),), 3: ((1, 1),)},
    {1: ((3, 0), (2, 1)), 0: ((2, 1),), 3: ((2, 1),)},
    {2: ((3, 1),), 0: ((3, 1),), 1: ((3, 1),)},
)


def spread(targets, inner):
    return [(row, e) for row, aside in targets for e in (range(1, inner) if aside else (0,))]


def targets_of(row, inner):
    near = set(spread(FIRST[row], inner))
    for found in RELAYS[row].values():
        near |= set(spread(found, inner))
    return near


def store_kernel(*refs):
    count = len(refs) // 2
    sem = refs[-1]
    copies = [pltpu.make_async_copy(refs[i], refs[count + i], sem.at[i]) for i in range(count)]
    for copy in copies:
        copy.start()
    for copy in copies:
        copy.wait()


def kernel(cfg, vis_hbm, coh_hbm, pairs_hbm, gains_hbm, duals_hbm, poly_hbm,
           gains_out, duals_out, poly_out,
           mixed, data, hot, tall, terms, early, jones, taken, pull, vis_ref, coh_ref, pairs_ref, gains_ref, duals_ref, poly_ref,
           tm_send, tm_recv, far, fq_send, fq_recv, load_sem):
    F, K, S, nt, nf, inner, chunks, terms_poly = cfg
    CH = S // chunks
    C = 8 * K
    parts = mixed.shape[2]
    tm = lax.axis_index("tm")
    fq = lax.axis_index("freq")
    z, y = tm // inner, tm % inner
    partner = fq + 1 - 2 * (fq % 2)
    MESH = pl.DeviceIdType.MESH
    columns_apart = range(1, inner)
    others = range(1, nf // 2)

    def role(act):
        for row in range(OUTER):
            pl.when(z == row)(lambda row=row: act(row))

    def chosen(table):
        found = table[0]
        for row in range(1, OUTER):
            found = jnp.where(z == row, table[row], found)
        return found

    nth = [chosen([SOURCES[row][k] for row in range(OUTER)]) for k in range(OUTER - 1)]

    def at(row, e):
        return row * inner + (y + e) % inner

    line = lambda k: (0, k)
    side = lambda k: (1, k)
    places = [("own", 0)]
    for group in ("mates", line(0), line(1), side(0), line(2), side(1), side(2)):
        places += [(group, e) for _, e in spread(((0, group == "mates" or group[0]),), inner)]
    blocks = [at(nth[group[1]] if isinstance(group, tuple) else z, e) for group, e in places]
    until = lambda group: [other for other, _ in places].index(group)

    def across(fq, d):
        there = (fq + 2 * d) % nf
        return there + 1 - 2 * (there % 2)

    barrier = pltpu.get_barrier_semaphore()

    def greet(peer):
        pl.semaphore_signal(barrier, inc=1, device_id=peer, device_id_type=MESH)

    def greet_rows(row):
        for other in range(OUTER):
            for there, e in sorted(targets_of(other, inner)):
                if there == row:
                    greet({"tm": at(other, inner - e)})

    role(greet_rows)
    greet({"freq": partner})
    for d in others:
        greet({"freq": across(fq, d)})

    loads = [pltpu.make_async_copy(src, dst, load_sem.at[i]) for i, (src, dst) in enumerate(
        ((coh_hbm, coh_ref), (vis_hbm, vis_ref), (pairs_hbm, pairs_ref),
         (gains_hbm, gains_ref), (duals_hbm, duals_ref), (poly_hbm, poly_ref)))]
    for load in loads:
        load.start()
    near = chosen([len(targets_of(row, inner)) for row in range(OUTER)])
    pl.semaphore_wait(barrier, near + 1 + (nf // 2 - 1))

    def greet_far(row):
        for other in range(OUTER):
            for there, _ in AFTER[other]:
                if there == row:
                    pl.semaphore_signal(far, inc=1, device_id={"tm": at(other, 0)}, device_id_type=MESH)

    role(greet_far)
    for load in loads[:3]:
        load.wait()
    data[tm, 0, 0:8, :] = jnp.zeros((8, LANES), jnp.float32)
    data[tm, 0, 0:2, :] = pairs_ref[...].astype(jnp.float32)
    for f in range(F):
        data[tm, f, 8:16, :] = vis_ref[f]
        data[tm, f, 16:, :] = coh_ref[f].astype(jnp.float32).reshape(C, LANES)

    def tm_copy(block, f, slot, device):
        rows = pl.ds(0, 16 + C) if f == 0 else pl.ds(8, 8 + C)
        return pltpu.make_async_remote_copy(
            src_ref=data.at[block, f, rows], dst_ref=data.at[block, f, rows],
            send_sem=tm_send.at[slot], recv_sem=tm_recv.at[block, f],
            device_id={"tm": device}, device_id_type=MESH)

    def arrived(block, f):
        tm_copy(block, f, 0, at(z, 1)).wait_recv()

    sends = []
    row_sends = [[] for _ in range(OUTER)]

    def send(row, source, f, targets):
        for there, e in spread(targets, inner):
            tm_copy(at(source, 0), f, len(row_sends[row]), at(there, e)).start()
            row_sends[row].append((source, f, there, e))

    def accept_one(row, group, f):
        source, aside = (row, 1) if group == "mates" else (SOURCES[row][group[1]], group[0])
        for _, e in spread(((source, aside),), inner):
            arrived(at(source, e), f)
            if not aside:
                send(row, source, f, relays(row, source, f))

    def accept(group, f):
        def act(row):
            if group == "pair":
                both = [(line(1), 0)] + [(line(0), g) for g in range(1, F)]
                for one in both[::-1] if row in (0,) else both:
                    accept_one(row, *one)
            else:
                accept_one(row, group, f)

        role(act)

    def relays(row, source, f):
        return RELAYS[row].get(source, ())

    stations = lax.broadcasted_iota(jnp.int32, (S, LANES), 0).astype(jnp.float32)

    across_stations = lax.broadcasted_iota(jnp.int32, (LANES, S), 1).astype(jnp.float32)

    def columns(place, half):
        return pl.ds((2 * place + half) * LANES, LANES)

    def make_hot(place):
        block = blocks[place]
        for half in range(2):
            row = data[block, 0, half : half + 1, :]
            hot[:, columns(place, half)] = jnp.where(stations == row, 1.0, 0.0).astype(jnp.bfloat16)
        turned = data[block, 0, 0:8, :].T
        for half in range(2):
            tall[columns(place, half), :] = jnp.where(across_stations == turned[:, half : half + 1], 1.0, 0.0).astype(jnp.bfloat16)

    def load_gains(gains, f):
        high, low = halves(gains[f].reshape(C, S))
        jones[2 * f * C : (2 * f + 1) * C, :] = high
        jones[(2 * f + 1) * C : (2 * f + 2) * C, :] = low

    def gather(place, first, last):
        both = pl.ds(place * 2 * LANES, 2 * LANES)
        found = jnp.dot(jones[2 * first * C : 2 * last * C, :], hot[:, both], preferred_element_type=jnp.float32)
        for f in range(first, last):
            base = 2 * (f - first) * C
            taken[place, f] = found[base : base + C] + found[base + C : base + 2 * C]

    def rows_sums(place, f):
        block = blocks[place]
        first = split([taken[place, f, c * K : (c + 1) * K, :LANES] for c in range(8)])
        second = split([taken[place, f, c * K : (c + 1) * K, LANES:] for c in range(8)])
        sky = split([data[block, f, 16 + c * K : 16 + (c + 1) * K, :] for c in range(8)])
        left = product(first, sky)
        right = product_right_adjoint(sky, second)
        model = product_right_adjoint(left, second)
        model = model[0] + model[1]
        residual = []
        for c in range(8):
            seen = data[block, f, 8 + c : 9 + c, :]
            residual.append(jnp.broadcast_to(seen - jnp.sum(model[c], axis=0, keepdims=True), (K, LANES)))
        residual = split(residual)
        ends = []
        out = product_right_adjoint(residual, right)
        ends.append(out[0] + out[1] + list(normal(right[0], right[1], ((0, 1), (2, 3)))))
        out = product_left_adjoint(residual, left)
        top, bottom, real, imag = normal(left[0], left[1], ((0, 2), (1, 3)))
        ends.append(out[0] + out[1] + [top, bottom, real, -imag])
        for half in range(2):
            high, low = halves(jnp.concatenate(ends[half], axis=0))
            terms[f, : 12 * K, columns(place, half)] = high
            terms[f, 12 * K :, columns(place, half)] = low

    bases = local_bases(F, nf)

    def pulls(f):
        for c in range(8):
            prior = from_basis(bases, f, [poly_ref[j, c] for j in range(terms_poly)])
            pull[f, c] = RHO * prior - duals_ref[f, c]

    def scattered(f, places, lanes):
        some = slice(places[0] * 2 * LANES, places[1] * 2 * LANES)
        sums = jnp.dot(terms[f, :, some], tall[some, lanes], preferred_element_type=jnp.float32)
        return sums[: 12 * K] + sums[12 * K :]

    def update(source, f, damping, chunk, done):
        lanes = slice(chunk * CH, (chunk + 1) * CH)
        sums = scattered(f, (done, nt), lanes)
        if done:
            sums = sums + early[f, :, lanes]
        part = [sums[c * K : (c + 1) * K] for c in range(12)]
        old, step = [], []
        for c in range(8):
            gain = source[f, c, :, lanes]
            old.append(gain)
            step.append(part[c] + pull[f, c, :, lanes] - RHO * gain)
        top, bottom, real, imag = part[8:]
        shift = damping * 0.5 * (top + bottom) + RHO
        upper, lower = top + shift, bottom + shift
        scale = 1.0 / (upper * lower - real * real - imag * imag)
        a, d, br, bi = lower * scale, upper * scale, -real * scale, -imag * scale
        sr, si = split(step)
        for row in range(2):
            p, q = 2 * row, 2 * row + 1
            gains_out[f, p, :, lanes] = old[p] + sr[p] * a + sr[q] * br + si[q] * bi
            gains_out[f, p + 4, :, lanes] = old[p + 4] + si[p] * a + si[q] * br - sr[q] * bi
            gains_out[f, q, :, lanes] = old[q] + sr[p] * br - si[p] * bi + sr[q] * d
            gains_out[f, q + 4, :, lanes] = old[q + 4] + si[p] * br + sr[p] * bi + si[q] * d

    def take(place, f):
        if f == 0:
            make_hot(place)
            gather(place, 0, F)
        rows_sums(place, f)

    def fq_copy(owner, f, chunk, slot, device):
        return pltpu.make_async_remote_copy(
            src_ref=mixed.at[owner, f, chunk], dst_ref=mixed.at[owner, f, chunk],
            send_sem=fq_send.at[slot, f, chunk], recv_sem=fq_recv.at[owner, f, chunk],
            device_id={"freq": device}, device_id_type=MESH)

    def fq_start(owner, f, chunk, slot, device):
        copy = fq_copy(owner, f, chunk, slot, device)
        copy.start()
        sends.append(copy)

    def sum_early(f, done):
        early[f] = scattered(f, (0, done), slice(0, S))

    def finish(f, done):
        for chunk in range(chunks):
            update(gains_ref, f, 12.0, chunk, done)
        for step in range(1, ITERS):
            load_gains(gains_out, f)

            for place in range(nt):
                gather(place, f, f + 1)
            for place in range(nt):
                rows_sums(place, f)

            for chunk in range(chunks):
                update(gains_out, f, 12.0 * 0.5**step, chunk, 0)
        for part in range(parts):
            some = slice(part * 8 // parts, (part + 1) * 8 // parts)
            value = gains_out[f, some] + duals_ref[f, some] * (1.0 / RHO)
            mixed[fq, f, part] = value.reshape(C // parts, S)
            for d in others:
                fq_start(fq, f, part, d, across(fq, d))
        for part in range(parts):
            fq_start(fq, f, part, 0, partner)

    def forward(f):
        for chunk in range(parts):
            for d in others:
                owner = across(fq, nf // 2 - d)
                fq_copy(owner, f, chunk, 0, partner).wait_recv()
                fq_start(owner, f, chunk, nf // 2 + d, partner)

    weights = basis_weights(F * nf)

    def received(f, chunk):
        fq_copy(partner, f, chunk, 0, partner).wait_recv()
        for d in others:
            fq_copy(across(partner, nf // 2 - d), f, chunk, 0, partner).wait_recv()

    def fit(f, part):
        for c in range(part * 8 // parts, (part + 1) * 8 // parts):
            base = (c - part * 8 // parts) * K
            values = [mixed[n, f, part, base : base + K, :] for n in range(nf)]
            coefficients = []
            for j in range(terms_poly):
                total = float(weights[j, f]) * values[0]
                for n in range(1, nf):
                    total = total + float(weights[j, n * F + f]) * values[n]
                if f > 0:
                    total = total + poly_out[j, c]
                poly_out[j, c] = total
                coefficients.append(total)
            if f == F - 1:
                for g in range(F):
                    prior = from_basis(bases, g, coefficients)
                    duals_out[g, c] = duals_ref[g, c] + RHO * (gains_out[g, c] - prior)

    later = range(1, F)
    def send_first(row):
        for f in range(F):
            send(row, row, f, FIRST[row])

    role(send_first)

    loads[3].wait()
    for f in range(F):
        load_gains(gains_ref, f)
    for f in range(F):
        take(0, f)

    def send_after(row):
        if AFTER[row]:
            pl.semaphore_wait(far, len(AFTER[row]))
            for f in range(F):
                send(row, row, f, AFTER[row])

    role(send_after)
    loads[4].wait()
    loads[5].wait()
    for f in range(F):
        pulls(f)

    arrivals = [("mates", 0), (line(0), 0)]
    for f in later:
        arrivals += [("mates", f)]
    arrivals += [("pair", 0)]
    for f in later:
        arrivals += [(line(1), f)]
    arrivals += [(side(0), 0), (line(2), 0)]
    arrivals += [(side(1), 0)]
    for f in later:
        arrivals += [(line(2), f)]
    arrivals += [(side(2), 0)]
    for f in later:
        arrivals += [(side(0), f)]
    for f in later:
        arrivals += [(side(1), f), (side(2), f)]

    def have(group, f):
        while (group, f) in arrivals:
            accept(*arrivals.pop(0))
        for place, (other, _) in enumerate(places):
            if other == group:
                take(place, f)

    have("mates", 0)
    have(line(0), 0)
    for f in later:
        have("mates", f)
    have("pair", 0)
    have(line(1), 0)
    for f in later:
        have(line(0), f)
        have(line(1), f)
    have(side(0), 0)
    have(line(2), 0)
    have(side(1), 0)
    sum_early(0, until(side(2)))
    have(side(2), 0)
    for f in later:
        have(line(2), f)
        have(side(0), f)
    for f in later:
        sum_early(f, until(side(1)))
    finish(0, until(side(2)))
    for f in later:
        have(side(1), f)
        have(side(2), f)
        finish(f, until(side(1)))
        forward(f - 1)
        for part in range(parts):
            received(f - 1, part)
            fit(f - 1, part)
    forward(F - 1)
    for part in range(parts):
        received(F - 1, part)
        fit(F - 1, part)
    for copy in sends:
        copy.wait_send()

    def drain(row):
        for slot, (source, f, there, e) in enumerate(row_sends[row]):
            tm_copy(at(source, 0), f, slot, at(there, e)).wait_send()

    role(drain)


def solution(mesh):
    nt, nf = mesh.shape["tm"], mesh.shape["freq"]

    def shards(*operands):
        visibilities, coherencies, pairs, gains_start, _, poly_start = operands
        F, _, K, S = gains_start.shape
        inner = nt // OUTER
        chunks, parts = 1, 2
        C = 8 * K
        cfg = (F, K, S, nt, nf, inner, chunks, poly_start.shape[0])
        wide = lambda x: pltpu.VMEM(x.shape, jnp.float32)
        vmem = pl.BlockSpec(memory_space=pltpu.VMEM)
        hbm = pl.BlockSpec(memory_space=pltpu.HBM)
        results = (gains_start, gains_start, poly_start)
        shapes = tuple(jax.ShapeDtypeStruct(x.shape, jnp.float32) for x in results)
        held = pl.pallas_call(
            partial(kernel, cfg),
            out_shape=shapes,
            in_specs=[hbm] * 6,
            out_specs=(vmem,) * 3,
            scratch_shapes=[
                pltpu.VMEM((nf, F, parts, C // parts, S), jnp.float32),
                pltpu.VMEM((nt, F, 16 + C, LANES), jnp.float32),
                pltpu.VMEM((S, nt * 2 * LANES), jnp.bfloat16),
                pltpu.VMEM((nt * 2 * LANES, S), jnp.bfloat16),
                pltpu.VMEM((F, 2 * 12 * K, nt * 2 * LANES), jnp.bfloat16),
                pltpu.VMEM((F, 12 * K, S), jnp.float32),
                pltpu.VMEM((2 * F * C, S), jnp.bfloat16),
                pltpu.VMEM((nt, F, C, 2 * LANES), jnp.float32),
                wide(gains_start),
                pltpu.VMEM(visibilities.shape, jnp.float32),
                pltpu.VMEM(coherencies.shape, jnp.bfloat16),
                pltpu.VMEM(pairs.shape, jnp.int32),
                wide(gains_start),
                wide(gains_start),
                wide(poly_start),
                pltpu.SemaphoreType.DMA((2 * OUTER * inner * F,)),
                pltpu.SemaphoreType.DMA((nt, F)),
                pltpu.SemaphoreType.REGULAR,
                pltpu.SemaphoreType.DMA((nf + 1, F, parts)),
                pltpu.SemaphoreType.DMA((nf, F, parts)),
                pltpu.SemaphoreType.DMA((6,)),
            ],
            compiler_params=pltpu.CompilerParams(collective_id=0, has_side_effects=True,
                                                 vmem_limit_bytes=40 * 2**20),
        )(*(pltpu.with_memory_space_constraint(x, pltpu.HBM) for x in operands))
        return pl.pallas_call(
            store_kernel,
            out_shape=shapes,
            in_specs=[vmem] * 3,
            out_specs=(hbm,) * 3,
            scratch_shapes=[pltpu.SemaphoreType.DMA((3,))],
            compiler_params=pltpu.CompilerParams(vmem_limit_bytes=16 * 2**20),
        )(*held)

    placed = (
        P("freq", None, "tm"),
        P("freq", None, None, "tm"),
        P(None, "tm"),
        P("freq", None, None, None),
        P("freq", None, None, None),
        P(),
    )
    return jax.shard_map(
        shards,
        mesh=mesh,
        in_specs=placed,
        out_specs=(P("freq", None, None, None), P("freq", None, None, None), P()),
        check_vma=False,
    )
```

```python
from functools import partial

import jax
import jax.numpy as jnp
import numpy as np
from jax import lax
from jax.experimental import pallas as pl
from jax.experimental.pallas import tpu as pltpu
from jax.sharding import PartitionSpec as P

ITERS = 2
RHO = 16.0
LANES = 128
OUTER = 4


def split(block):
    return ([block[i] for i in range(4)], [block[i + 4] for i in range(4)])


def product(left, right):
    lr, li = left
    rr, ri = right
    out_real, out_imag = [], []
    for row in range(2):
        for col in range(2):
            a, b = 2 * row, 2 * row + 1
            out_real.append(lr[a] * rr[col] - li[a] * ri[col] + lr[b] * rr[col + 2] - li[b] * ri[col + 2])
            out_imag.append(lr[a] * ri[col] + li[a] * rr[col] + lr[b] * ri[col + 2] + li[b] * rr[col + 2])
    return (out_real, out_imag)


def product_right_adjoint(left, right):
    lr, li = left
    rr, ri = right
    out_real, out_imag = [], []
    for row in range(2):
        for col in range(2):
            a, b, c, d = 2 * row, 2 * row + 1, 2 * col, 2 * col + 1
            out_real.append(lr[a] * rr[c] + li[a] * ri[c] + lr[b] * rr[d] + li[b] * ri[d])
            out_imag.append(li[a] * rr[c] - lr[a] * ri[c] + li[b] * rr[d] - lr[b] * ri[d])
    return (out_real, out_imag)


def product_left_adjoint(left, right):
    lr, li = left
    rr, ri = right
    out_real, out_imag = [], []
    for row in range(2):
        for col in range(2):
            a, b, c, d = row, row + 2, col, col + 2
            out_real.append(lr[a] * rr[c] + li[a] * ri[c] + lr[b] * rr[d] + li[b] * ri[d])
            out_imag.append(lr[a] * ri[c] - li[a] * rr[c] + lr[b] * ri[d] - li[b] * rr[d])
    return (out_real, out_imag)


def normal(r, i, rows):
    (a, b), (c, d) = rows
    top = r[a] * r[a] + i[a] * i[a] + r[b] * r[b] + i[b] * i[b]
    bottom = r[c] * r[c] + i[c] * i[c] + r[d] * r[d] + i[d] * i[d]
    real = r[a] * r[c] + i[a] * i[c] + r[b] * r[d] + i[b] * i[d]
    imag = i[a] * r[c] - r[a] * i[c] + i[b] * r[d] - r[b] * i[d]
    return top, bottom, real, imag


def basis_weights(count):
    x = (2.0 * np.arange(count, dtype=np.float64) + 1.0) / count - 1.0
    basis = np.stack([np.ones_like(x), x, 1.5 * x * x - 0.5, 2.5 * x * x * x - 1.5 * x], axis=1)
    return np.linalg.solve(basis.T @ basis, basis.T)


def halves(value):
    high = value.astype(jnp.bfloat16)
    return high, (value - high.astype(jnp.float32)).astype(jnp.bfloat16)


def from_basis(bases, f, coefficients):
    total = coefficients[0]
    for j in range(1, len(coefficients)):
        total = total + bases[f][j] * coefficients[j]
    return total


def local_bases(F, nf):
    bases = []
    for f in range(F):
        channel = (lax.axis_index("freq") * F + f).astype(jnp.float32)
        x = (2.0 * channel + 1.0) / (F * nf) - 1.0
        bases.append([None, x, 1.5 * x * x - 0.5, 2.5 * x * x * x - 1.5 * x])
    return bases


SOURCES = ((1, 3, 2), (0, 2, 3), (1, 0, 3), (2, 0, 1))
FIRST = (
    ((1, 0), (0, 1), (2, 0)),
    ((0, 0), (1, 1), (2, 0)),
    ((1, 0), (2, 1), (3, 0)),
    ((0, 0), (3, 1), (1, 0), (2, 0)),
)
AFTER = (((3, 0),), (), (), ())
RELAYS = (
    {1: ((0, 1),), 3: ((0, 1),)},
    {2: ((0, 0), (1, 1), (0, 1)), 0: ((1, 1),), 3: ((1, 1),)},
    {1: ((3, 0), (2, 1)), 0: ((2, 1),), 3: ((2, 1),)},
    {2: ((3, 1),), 0: ((3, 1),), 1: ((3, 1),)},
)


def spread(targets, inner):
    return [(row, e) for row, aside in targets for e in (range(1, inner) if aside else (0,))]


def targets_of(row, inner):
    near = set(spread(FIRST[row], inner))
    for found in RELAYS[row].values():
        near |= set(spread(found, inner))
    return near


def store_kernel(*refs):
    count = len(refs) // 2
    sem = refs[-1]
    copies = [pltpu.make_async_copy(refs[i], refs[count + i], sem.at[i]) for i in range(count)]
    for copy in copies:
        copy.start()
    for copy in copies:
        copy.wait()


def kernel(cfg, vis_hbm, coh_hbm, pairs_hbm, gains_hbm, duals_hbm, poly_hbm,
           gains_out, duals_out, poly_out,
           mixed, data, hot, tall, terms, early, jones, taken, pull, vis_ref, coh_ref, pairs_ref, gains_ref, duals_ref, poly_ref,
           tm_send, tm_recv, far, fq_send, fq_recv, load_sem):
    F, K, S, nt, nf, inner, chunks, terms_poly = cfg
    CH = S // chunks
    C = 8 * K
    parts = mixed.shape[2]
    tm = lax.axis_index("tm")
    fq = lax.axis_index("freq")
    z, y = tm // inner, tm % inner
    partner = fq + 1 - 2 * (fq % 2)
    MESH = pl.DeviceIdType.MESH
    columns_apart = range(1, inner)
    others = range(1, nf // 2)

    def role(act):
        for row in range(OUTER):
            pl.when(z == row)(lambda row=row: act(row))

    def chosen(table):
        found = table[0]
        for row in range(1, OUTER):
            found = jnp.where(z == row, table[row], found)
        return found

    nth = [chosen([SOURCES[row][k] for row in range(OUTER)]) for k in range(OUTER - 1)]

    def at(row, e):
        return row * inner + (y + e) % inner

    line = lambda k: (0, k)
    side = lambda k: (1, k)
    places = [("own", 0)]
    for group in ("mates", line(0), line(1), side(0), line(2), side(1), side(2)):
        places += [(group, e) for _, e in spread(((0, group == "mates" or group[0]),), inner)]
    blocks = [at(nth[group[1]] if isinstance(group, tuple) else z, e) for group, e in places]
    until = lambda group: [other for other, _ in places].index(group)

    def across(fq, d):
        there = (fq + 2 * d) % nf
        return there + 1 - 2 * (there % 2)

    barrier = pltpu.get_barrier_semaphore()

    def greet(peer):
        pl.semaphore_signal(barrier, inc=1, device_id=peer, device_id_type=MESH)

    def greet_rows(row):
        for other in range(OUTER):
            for there, e in sorted(targets_of(other, inner)):
                if there == row:
                    greet({"tm": at(other, inner - e)})

    role(greet_rows)
    greet({"freq": partner})
    for d in others:
        greet({"freq": across(fq, d)})

    loads = [pltpu.make_async_copy(src, dst, load_sem.at[i]) for i, (src, dst) in enumerate(
        ((coh_hbm, coh_ref), (vis_hbm, vis_ref), (pairs_hbm, pairs_ref),
         (gains_hbm, gains_ref), (duals_hbm, duals_ref), (poly_hbm, poly_ref)))]
    for load in loads:
        load.start()
    near = chosen([len(targets_of(row, inner)) for row in range(OUTER)])
    pl.semaphore_wait(barrier, near + 1 + (nf // 2 - 1))

    def greet_far(row):
        for other in range(OUTER):
            for there, _ in AFTER[other]:
                if there == row:
                    pl.semaphore_signal(far, inc=1, device_id={"tm": at(other, 0)}, device_id_type=MESH)

    role(greet_far)
    for load in loads[:3]:
        load.wait()
    data[tm, 0, 0:8, :] = jnp.zeros((8, LANES), jnp.float32)
    data[tm, 0, 0:2, :] = pairs_ref[...].astype(jnp.float32)
    for f in range(F):
        data[tm, f, 8:16, :] = vis_ref[f]
        data[tm, f, 16:, :] = coh_ref[f].astype(jnp.float32).reshape(C, LANES)

    def tm_copy(block, f, slot, device):
        rows = pl.ds(0, 16 + C) if f == 0 else pl.ds(8, 8 + C)
        return pltpu.make_async_remote_copy(
            src_ref=data.at[block, f, rows], dst_ref=data.at[block, f, rows],
            send_sem=tm_send.at[slot], recv_sem=tm_recv.at[block, f],
            device_id={"tm": device}, device_id_type=MESH)

    def arrived(block, f):
        tm_copy(block, f, 0, at(z, 1)).wait_recv()

    sends = []
    row_sends = [[] for _ in range(OUTER)]

    def send(row, source, f, targets):
        for there, e in spread(targets, inner):
            tm_copy(at(source, 0), f, len(row_sends[row]), at(there, e)).start()
            row_sends[row].append((source, f, there, e))

    def accept_one(row, group, f):
        source, aside = (row, 1) if group == "mates" else (SOURCES[row][group[1]], group[0])
        for _, e in spread(((source, aside),), inner):
            arrived(at(source, e), f)
            if not aside:
                send(row, source, f, relays(row, source, f))

    def accept(group, f):
        def act(row):
            if group == "pair":
                both = [(line(1), 0)] + [(line(0), g) for g in range(1, F)]
                for one in both[::-1] if row in (0,) else both:
                    accept_one(row, *one)
            else:
                accept_one(row, group, f)

        role(act)

    def relays(row, source, f):
        return RELAYS[row].get(source, ())

    sixteen = lax.broadcasted_iota(jnp.int32, (16, LANES), 0).astype(jnp.float32)
    lane = lax.broadcasted_iota(jnp.int32, (LANES, LANES), 1).astype(jnp.float32)

    def columns(place, half):
        return pl.ds((2 * place + half) * LANES, LANES)

    def make_hot(place):
        block = blocks[place]
        few = 16
        zero = jnp.zeros((few, LANES), jnp.bfloat16)
        for half in range(2):
            row = data[block, 0, half : half + 1, :]
            tens = jnp.floor(row * (1.0 / few))
            units = jnp.broadcast_to(row - few * tens, (few, LANES))
            tens = jnp.broadcast_to(tens, (few, LANES)).astype(jnp.bfloat16)
            unit = jnp.where(sixteen == units, 1.0, 0.0).astype(jnp.bfloat16)
            for i in range(S // few):
                hot[i * few : (i + 1) * few, columns(place, half)] = jnp.where(tens == jnp.bfloat16(i), unit, zero)
        turned = data[block, 0, 0:8, :].T
        zero = jnp.zeros((LANES, LANES), jnp.bfloat16)
        for half in range(2):
            column = jnp.broadcast_to(turned[:, half : half + 1], (LANES, LANES))
            tile = jnp.floor(column * (1.0 / LANES))
            unit = jnp.where(lane == column - LANES * tile, 1.0, 0.0).astype(jnp.bfloat16)
            tile = tile.astype(jnp.bfloat16)
            for i in range(S // LANES):
                tall[columns(place, half), i * LANES : (i + 1) * LANES] = jnp.where(tile == jnp.bfloat16(i), unit, zero)

    def load_gains(gains, f):
        high, low = halves(gains[f].reshape(C, S))
        jones[2 * f * C : (2 * f + 1) * C, :] = high
        jones[(2 * f + 1) * C : (2 * f + 2) * C, :] = low

    def gather(place, first, last):
        both = pl.ds(place * 2 * LANES, 2 * LANES)
        found = jnp.dot(jones[2 * first * C : 2 * last * C, :], hot[:, both], preferred_element_type=jnp.float32)
        for f in range(first, last):
            base = 2 * (f - first) * C
            taken[place, f] = found[base : base + C] + found[base + C : base + 2 * C]

    def rows_sums(place, f):
        block = blocks[place]
        first = split([taken[place, f, c * K : (c + 1) * K, :LANES] for c in range(8)])
        second = split([taken[place, f, c * K : (c + 1) * K, LANES:] for c in range(8)])
        sky = split([data[block, f, 16 + c * K : 16 + (c + 1) * K, :] for c in range(8)])
        left = product(first, sky)
        right = product_right_adjoint(sky, second)
        model = product_right_adjoint(left, second)
        model = model[0] + model[1]
        residual = []
        for c in range(8):
            seen = data[block, f, 8 + c : 9 + c, :]
            residual.append(jnp.broadcast_to(seen - jnp.sum(model[c], axis=0, keepdims=True), (K, LANES)))
        residual = split(residual)
        ends = []
        out = product_right_adjoint(residual, right)
        ends.append(out[0] + out[1] + list(normal(right[0], right[1], ((0, 1), (2, 3)))))
        out = product_left_adjoint(residual, left)
        top, bottom, real, imag = normal(left[0], left[1], ((0, 2), (1, 3)))
        ends.append(out[0] + out[1] + [top, bottom, real, -imag])
        for half in range(2):
            high, low = halves(jnp.concatenate(ends[half], axis=0))
            terms[f, : 12 * K, columns(place, half)] = high
            terms[f, 12 * K :, columns(place, half)] = low

    bases = local_bases(F, nf)

    def pulls(f):
        for c in range(8):
            prior = from_basis(bases, f, [poly_ref[j, c] for j in range(terms_poly)])
            pull[f, c] = RHO * prior - duals_ref[f, c]

    def scattered(f, places, lanes):
        some = slice(places[0] * 2 * LANES, places[1] * 2 * LANES)
        sums = jnp.dot(terms[f, :, some], tall[some, lanes], preferred_element_type=jnp.float32)
        return sums[: 12 * K] + sums[12 * K :]

    def update(source, f, damping, chunk, done):
        lanes = slice(chunk * CH, (chunk + 1) * CH)
        sums = scattered(f, (done, nt), lanes)
        if done:
            sums = sums + early[f, :, lanes]
        part = [sums[c * K : (c + 1) * K] for c in range(12)]
        old, step = [], []
        for c in range(8):
            gain = source[f, c, :, lanes]
            old.append(gain)
            step.append(part[c] + pull[f, c, :, lanes] - RHO * gain)
        top, bottom, real, imag = part[8:]
        shift = damping * 0.5 * (top + bottom) + RHO
        upper, lower = top + shift, bottom + shift
        scale = 1.0 / (upper * lower - real * real - imag * imag)
        a, d, br, bi = lower * scale, upper * scale, -real * scale, -imag * scale
        sr, si = split(step)
        for row in range(2):
            p, q = 2 * row, 2 * row + 1
            gains_out[f, p, :, lanes] = old[p] + sr[p] * a + sr[q] * br + si[q] * bi
            gains_out[f, p + 4, :, lanes] = old[p + 4] + si[p] * a + si[q] * br - sr[q] * bi
            gains_out[f, q, :, lanes] = old[q] + sr[p] * br - si[p] * bi + sr[q] * d
            gains_out[f, q + 4, :, lanes] = old[q + 4] + si[p] * br + sr[p] * bi + si[q] * d

    def take(place, f):
        if f == 0:
            make_hot(place)
            gather(place, 0, F)
        rows_sums(place, f)

    def fq_copy(owner, f, chunk, slot, device):
        return pltpu.make_async_remote_copy(
            src_ref=mixed.at[owner, f, chunk], dst_ref=mixed.at[owner, f, chunk],
            send_sem=fq_send.at[slot, f, chunk], recv_sem=fq_recv.at[owner, f, chunk],
            device_id={"freq": device}, device_id_type=MESH)

    def fq_start(owner, f, chunk, slot, device):
        copy = fq_copy(owner, f, chunk, slot, device)
        copy.start()
        sends.append(copy)

    def sum_early(f, done):
        early[f] = scattered(f, (0, done), slice(0, S))

    def finish(f, done):
        for chunk in range(chunks):
            update(gains_ref, f, 12.0, chunk, done)
        for step in range(1, ITERS):
            load_gains(gains_out, f)

            for place in range(nt):
                gather(place, f, f + 1)
            for place in range(nt):
                rows_sums(place, f)

            for chunk in range(chunks):
                update(gains_out, f, 12.0 * 0.5**step, chunk, 0)
        for part in range(parts):
            some = slice(part * 8 // parts, (part + 1) * 8 // parts)
            value = gains_out[f, some] + duals_ref[f, some] * (1.0 / RHO)
            mixed[fq, f, part] = value.reshape(C // parts, S)
            for d in others:
                fq_start(fq, f, part, d, across(fq, d))
        for part in range(parts):
            fq_start(fq, f, part, 0, partner)

    def forward(f):
        for chunk in range(parts):
            for d in others:
                owner = across(fq, nf // 2 - d)
                fq_copy(owner, f, chunk, 0, partner).wait_recv()
                fq_start(owner, f, chunk, nf // 2 + d, partner)

    weights = basis_weights(F * nf)

    def received(f, chunk):
        fq_copy(partner, f, chunk, 0, partner).wait_recv()
        for d in others:
            fq_copy(across(partner, nf // 2 - d), f, chunk, 0, partner).wait_recv()

    def fit(f, part):
        for c in range(part * 8 // parts, (part + 1) * 8 // parts):
            base = (c - part * 8 // parts) * K
            values = [mixed[n, f, part, base : base + K, :] for n in range(nf)]
            coefficients = []
            for j in range(terms_poly):
                total = float(weights[j, f]) * values[0]
                for n in range(1, nf):
                    total = total + float(weights[j, n * F + f]) * values[n]
                if f > 0:
                    total = total + poly_out[j, c]
                poly_out[j, c] = total
                coefficients.append(total)
            if f == F - 1:
                for g in range(F):
                    prior = from_basis(bases, g, coefficients)
                    duals_out[g, c] = duals_ref[g, c] + RHO * (gains_out[g, c] - prior)

    later = range(1, F)
    def send_first(row):
        for f in range(F):
            send(row, row, f, FIRST[row])

    role(send_first)

    loads[3].wait()
    for f in range(F):
        load_gains(gains_ref, f)
    for f in range(F):
        take(0, f)

    def send_after(row):
        if AFTER[row]:
            pl.semaphore_wait(far, len(AFTER[row]))
            for f in range(F):
                send(row, row, f, AFTER[row])

    role(send_after)
    loads[4].wait()
    loads[5].wait()
    for f in range(F):
        pulls(f)

    arrivals = [("mates", 0), (line(0), 0)]
    for f in later:
        arrivals += [("mates", f)]
    arrivals += [("pair", 0)]
    for f in later:
        arrivals += [(line(1), f)]
    arrivals += [(side(0), 0), (line(2), 0)]
    arrivals += [(side(1), 0)]
    for f in later:
        arrivals += [(line(2), f)]
    arrivals += [(side(2), 0)]
    for f in later:
        arrivals += [(side(0), f)]
    for f in later:
        arrivals += [(side(1), f), (side(2), f)]

    def have(group, f):
        while (group, f) in arrivals:
            accept(*arrivals.pop(0))
        for place, (other, _) in enumerate(places):
            if other == group:
                take(place, f)

    have("mates", 0)
    have(line(0), 0)
    for f in later:
        have("mates", f)
    have("pair", 0)
    have(line(1), 0)
    for f in later:
        have(line(0), f)
        have(line(1), f)
    have(side(0), 0)
    have(line(2), 0)
    have(side(1), 0)
    sum_early(0, until(side(2)))
    have(side(2), 0)
    for f in later:
        have(line(2), f)
        have(side(0), f)
    for f in later:
        sum_early(f, until(side(1)))
    finish(0, until(side(2)))
    for f in later:
        have(side(1), f)
        have(side(2), f)
        finish(f, until(side(1)))
        forward(f - 1)
        for part in range(parts):
            received(f - 1, part)
            fit(f - 1, part)
    forward(F - 1)
    for part in range(parts):
        received(F - 1, part)
        fit(F - 1, part)
    for copy in sends:
        copy.wait_send()

    def drain(row):
        for slot, (source, f, there, e) in enumerate(row_sends[row]):
            tm_copy(at(source, 0), f, slot, at(there, e)).wait_send()

    role(drain)


def solution(mesh):
    nt, nf = mesh.shape["tm"], mesh.shape["freq"]

    def shards(*operands):
        visibilities, coherencies, pairs, gains_start, _, poly_start = operands
        F, _, K, S = gains_start.shape
        inner = nt // OUTER
        chunks, parts = 1, 2
        C = 8 * K
        cfg = (F, K, S, nt, nf, inner, chunks, poly_start.shape[0])
        wide = lambda x: pltpu.VMEM(x.shape, jnp.float32)
        vmem = pl.BlockSpec(memory_space=pltpu.VMEM)
        hbm = pl.BlockSpec(memory_space=pltpu.HBM)
        results = (gains_start, gains_start, poly_start)
        shapes = tuple(jax.ShapeDtypeStruct(x.shape, jnp.float32) for x in results)
        held = pl.pallas_call(
            partial(kernel, cfg),
            out_shape=shapes,
            in_specs=[hbm] * 6,
            out_specs=(vmem,) * 3,
            scratch_shapes=[
                pltpu.VMEM((nf, F, parts, C // parts, S), jnp.float32),
                pltpu.VMEM((nt, F, 16 + C, LANES), jnp.float32),
                pltpu.VMEM((S, nt * 2 * LANES), jnp.bfloat16),
                pltpu.VMEM((nt * 2 * LANES, S), jnp.bfloat16),
                pltpu.VMEM((F, 2 * 12 * K, nt * 2 * LANES), jnp.bfloat16),
                pltpu.VMEM((F, 12 * K, S), jnp.float32),
                pltpu.VMEM((2 * F * C, S), jnp.bfloat16),
                pltpu.VMEM((nt, F, C, 2 * LANES), jnp.float32),
                wide(gains_start),
                pltpu.VMEM(visibilities.shape, jnp.float32),
                pltpu.VMEM(coherencies.shape, jnp.bfloat16),
                pltpu.VMEM(pairs.shape, jnp.int32),
                wide(gains_start),
                wide(gains_start),
                wide(poly_start),
                pltpu.SemaphoreType.DMA((2 * OUTER * inner * F,)),
                pltpu.SemaphoreType.DMA((nt, F)),
                pltpu.SemaphoreType.REGULAR,
                pltpu.SemaphoreType.DMA((nf + 1, F, parts)),
                pltpu.SemaphoreType.DMA((nf, F, parts)),
                pltpu.SemaphoreType.DMA((6,)),
            ],
            compiler_params=pltpu.CompilerParams(collective_id=0, has_side_effects=True,
                                                 vmem_limit_bytes=40 * 2**20),
        )(*(pltpu.with_memory_space_constraint(x, pltpu.HBM) for x in operands))
        return pl.pallas_call(
            store_kernel,
            out_shape=shapes,
            in_specs=[vmem] * 3,
            out_specs=(hbm,) * 3,
            scratch_shapes=[pltpu.SemaphoreType.DMA((3,))],
            compiler_params=pltpu.CompilerParams(vmem_limit_bytes=16 * 2**20),
        )(*held)

    placed = (
        P("freq", None, "tm"),
        P("freq", None, None, "tm"),
        P(None, "tm"),
        P("freq", None, None, None),
        P("freq", None, None, None),
        P(),
    )
    return jax.shard_map(
        shards,
        mesh=mesh,
        in_specs=placed,
        out_specs=(P("freq", None, None, None), P("freq", None, None, None), P()),
        check_vma=False,
    )
```
